256 devices in a mesh: det: 2 (over core), ord: 128 (over z, y, x).
Axes of the slice: x: 4, y: 4, z: 8, core: 2. Of those that a mesh axis runs over, the one named last changes fastest.
Arguments:
- wigner: bfloat16 [2048, 2, 128, 2048], P('ord', None, None, 'det'), may hold values from -0.125 to 0.125
- alm: bfloat16 [2048, 2, 2048], P('ord'), may hold values from -6 to 6
- beam: bfloat16 [64, 2, 2048], replicated, may hold values from -6 to 6
- crossing: int32 [128, 128], P('ord'), may hold values from 0 to 8191, as said below
- offsets: int32 [128, 4096], P('ord'), may hold values from 0 to 124
- fraction: float32 [128, 4096], P('ord'), may hold values from 0 to 1
- taps: float32 [33], replicated, may hold values from -1 to 1
Outputs:
- detector_signal: float32 [64, 524288], P('det', 'ord')
The draws below stay inside these ranges and needn't reach their ends.
Inputs may be any that keep to these rules, and one draw needn't show every extreme that they name: `crossing`: within one interval's 128 entries at most 2 lie in any one block of 64 consecutive ids; in every draw some block holds exactly 2 entries of every interval.
All inputs are finite; a program needn't handle non-finite values.
Results may differ from the reference program's by a relative error of at most 0.0057.
Values may be sent and summed in bfloat16 or wider, within the bound.
No kernel may reach another device: no remote copies, remote signals or barrier semaphores. Data moves between devices by JAX's collectives and lax.ppermute only.
A program may use at most 192 MiB of HBM per device.

```python
import math
import jax
import jax.numpy as jnp
from jax import lax

L = 2048
M_DEV = 16
K = 2
LATS = 128
TILE = 128
CROSSINGS = 128
SAMPLES = 32
REACH = 16
TAPS = 33
M = 2048
DETS = 64
INTERVALS = 128
TILES_DEV = 64
CAP = 2
TIME = 4096


def draw_crossing(key, part):
    entries = INTERVALS * CAP
    key_hot, key_score, key_order, key_local = jax.random.split(key, 4)
    hot_holder = jax.random.randint(key_hot, (), 0, INTERVALS)
    entry_ids = jnp.arange(entries, dtype=jnp.int32)
    holders = entry_ids // CAP
    scores = jax.random.randint(key_score, (INTERVALS, entries), 0, 1 << 20)
    first_row = jnp.arange(INTERVALS, dtype=jnp.int32)[:, None] == 0
    edge_entries = (entry_ids == 0) | (entry_ids == (INTERVALS - 1) * CAP)
    scores = jnp.where(first_row & edge_entries[None, :], -1, scores)
    scores = jnp.where(holders[None, :] == hot_holder, -2, scores)
    ranked = jnp.argsort(scores * entries + entry_ids[None, :], axis=1, stable=True)
    taken = ranked[:, :CROSSINGS]
    local_draws = jax.random.randint(key_local, (INTERVALS, entries), 0, TILES_DEV)
    local_draws = jnp.where(first_row & (entry_ids[None, :] == 0), 0, local_draws)
    local_draws = jnp.where(first_row & (entry_ids[None, :] == (INTERVALS - 1) * CAP), TILES_DEV - 1, local_draws)
    tile_ids = holders[None, :] * TILES_DEV + local_draws
    chosen = jnp.take_along_axis(tile_ids, taken, axis=1)
    order_scores = jax.random.randint(key_order, (INTERVALS, CROSSINGS), 0, 1 << 20) * CROSSINGS + jnp.arange(CROSSINGS, dtype=jnp.int32)[None, :]
    shuffle = jnp.argsort(order_scores, axis=1, stable=True)
    return jnp.take_along_axis(chosen, shuffle, axis=1).astype(jnp.int32)


def plant(values, key, low, largest):
    spot = [jax.random.randint(jax.random.fold_in(key, axis), (), 0, length) for axis, length in enumerate(values.shape)]
    longest = values.shape.index(max(values.shape))
    beside = spot[:longest] + [(spot[longest] + 1) % values.shape[longest]] + spot[longest + 1:]
    return values.at[tuple(spot)].set(low).at[tuple(beside)].set(largest)


def block_levels(rng, extent, shards, low, top_value):
    def one(dim, shards_of):
        draws = jax.random.uniform(jax.random.fold_in(jax.random.fold_in(rng, 6), dim), (shards_of,), jnp.float32, low / len(shards), top_value / len(shards))
        return jnp.repeat(jnp.exp(draws), extent[dim] // shards_of).reshape((-1,) + (1,) * (len(extent) - dim - 1))

    level = one(*shards[0])
    for cut in shards[1:]:
        level = level * one(*cut)
    return level


def bell_draw(rng, extent, width, most, shards=(), kind=jnp.bfloat16):
    values = jax.random.normal(rng, extent, jnp.float32) * width
    if len(shards) > 0:
        values = block_levels(rng, extent, shards, -0.22, 0.18) * values
    return jnp.clip(values, min=-most, max=most).astype(kind)


def setup_inputs(seed: int = 0) -> dict:
    streams_of = jax.random.split(jax.random.key(seed), 8)
    return {
        "wigner": bell_draw(streams_of[0], (M, K, LATS, L), L ** -0.5, 0.125, ((0, 128), (3, 2))),
        "alm": bell_draw(streams_of[1], (M, 2, L), 1.0, 6.0, ((0, 128),)),
        "beam": bell_draw(streams_of[2], (DETS, K, L), 1.0, 6.0),
        "crossing": draw_crossing(jax.random.fold_in(streams_of[7], 71), 0),
        "offsets": plant(jax.random.randint(streams_of[4], (INTERVALS, TIME), 0, TILE - 3), jax.random.fold_in(streams_of[4], 1), 0, (TILE - 3) - 1).astype(jnp.int32),
        "fraction": jnp.clip(1.0 * jax.random.uniform(streams_of[5], (INTERVALS, TIME), jnp.float32) ** block_levels(streams_of[5], (INTERVALS, TIME), ((0, 128),), -0.2, 0.2), 0.0, 1.0),
        "taps": bell_draw(streams_of[6], (TAPS,), TAPS ** -0.5, 1.0, (), jnp.float32),
    }


def lagrange_weights(position):
    shifted = position + 1.0
    minus_one = position - 1.0
    minus_two = position - 2.0
    return (-position * minus_one * minus_two / 6.0, shifted * minus_one * minus_two / 2.0, -shifted * position * minus_two / 2.0, shifted * position * minus_one / 6.0)

def reference(wigner, alm, beam, crossing, offsets, fraction, taps):
    orders = wigner.shape[0]
    groups = orders // M_DEV
    wigner_blocks = wigner.reshape(groups, M_DEV, K, LATS, L)
    alm_blocks = alm.reshape(groups, M_DEV, 2, L)
    beam_wide = beam.astype(jnp.float32)

    def spectra_block(operands):
        wigner_block, alm_block = operands
        coefficients = (beam_wide[:, None, :, None, :] * alm_block.astype(jnp.float32)[None, :, None, :, :]).astype(jnp.bfloat16)
        result = jnp.einsum('mkrl,jmkcl->jkrcm', wigner_block.astype(jnp.float32), coefficients.astype(jnp.float32), precision=lax.Precision.HIGHEST)
        return result.astype(jnp.bfloat16)
    spectra = lax.map(spectra_block, (wigner_blocks, alm_blocks))
    spectra = jnp.transpose(spectra, (2, 3, 1, 4, 0, 5)).reshape(K * LATS, DETS, 2, orders).astype(jnp.float32)
    longitudes = 2 * orders
    zero_column = jnp.zeros((K * LATS, DETS, 1), jnp.float32)
    real_part = jnp.concatenate([spectra[:, :, 0], zero_column], axis=2)
    imag_part = jnp.concatenate([spectra[:, :, 1], zero_column], axis=2)
    field = jnp.fft.irfft(real_part + 1j * imag_part, n=longitudes, axis=2) * (longitudes / math.sqrt(longitudes))
    cube = field.astype(jnp.bfloat16)
    blocks_per_item = longitudes // TILE

    def interval_samples(triple):
        wanted, offset_row, fraction_row = triple
        item = wanted // blocks_per_item
        start_column = wanted % blocks_per_item * TILE
        offset_rows = offset_row.reshape(CROSSINGS, SAMPLES)
        fraction_rows = fraction_row.reshape(CROSSINGS, SAMPLES)
        factors = lagrange_weights(fraction_rows)
        total = jnp.zeros((CROSSINGS, SAMPLES, DETS), jnp.float32)
        for place in range(4):
            columns = start_column[:, None] + offset_rows + place
            picked = cube[item[:, None], :, columns]
            total = total + factors[place][:, :, None] * picked.astype(jnp.float32)
        return jnp.transpose(total, (2, 0, 1)).reshape(DETS, CROSSINGS * SAMPLES).astype(jnp.bfloat16)
    samples = lax.map(interval_samples, (crossing, offsets, fraction))
    samples = jnp.transpose(samples, (1, 0, 2)).reshape(DETS, -1).astype(jnp.float32)
    padded = jnp.pad(samples, ((0, 0), (REACH, REACH)))
    span = samples.shape[1]
    signal = jnp.zeros_like(samples)
    for shift_index in range(TAPS):
        signal = signal + taps[shift_index] * padded[:, shift_index:shift_index + span]
    return signal
```

```python
import math

import jax
import jax.numpy as jnp
import numpy as np
from jax import lax
from jax.experimental import pallas as pl
from jax.experimental.pallas import tpu as pltpu
from jax.sharding import PartitionSpec as P

F32 = jnp.float32
BF16 = jnp.bfloat16
I32 = jnp.int32

ORD = 128
EPD = 16
ROWS = 9
DET = 32
NT = (((1,), (1,)), ((), ()))


def lanes_of(shape):
    return lax.broadcasted_iota(I32, shape, len(shape) - 1)


def spectra_kernel(place, wig, alm, beam, crossing, offsets, fraction, keep, send, flat, cells):
    g = pl.program_id(0)

    @pl.when(g == 0)
    def positions():
        c = crossing[...]
        holder = lax.shift_right_logical(c, 6)
        across = jnp.broadcast_to(holder, (128, 128)).astype(F32)
        down = jnp.transpose(across)
        sub = lax.broadcasted_iota(I32, (128, 128), 0)
        lane = lanes_of((128, 128))
        earlier = jnp.where((across == down) & (sub < lane), 1.0, 0.0)
        slot = jnp.sum(earlier, axis=0, keepdims=True).astype(I32)
        flat[...] = holder * 2 + slot
        o32 = offsets[...].astype(F32)
        f32_ = fraction[...]
        hi = f32_.astype(BF16).astype(F32)
        lo = f32_ - hi
        lane32 = lanes_of((32, 128))
        ids = jnp.broadcast_to((c & 63).astype(F32), (128, 128))
        ids = jnp.sum(jnp.where(sub == lane, ids, 0.0), axis=1, keepdims=True)
        for part in range(4):
            sh = 128 - 32 * part
            row = jnp.where(
                lane32 < 32,
                pltpu.roll(o32, sh % 128, 1),
                jnp.where(
                    lane32 < 64, pltpu.roll(hi, (sh + 32) % 128, 1), pltpu.roll(lo, (sh + 64) % 128, 1)
                ),
            )
            cells[pl.ds(part, 32, stride=4), :] = row
        data = jnp.where(lane < 96, cells[...], jnp.broadcast_to(ids, (128, 128))).astype(BF16)
        for s in range(2):
            pick = jnp.where((sub == holder) & (slot == s), 1.0, 0.0).astype(BF16)
            got = jnp.dot(pick, data, preferred_element_type=F32)
            keep[pl.ds(8 + 9 * s, 128, stride=18), :] = got
            send[pl.ds(8 + 9 * s, 128, stride=18), :] = jnp.zeros((128, 128), F32)

    lane = lanes_of((128, 128))
    first = jnp.where((place[1] == 0) & (g == 0), 1.0 / 64.0, 1.0 / 32.0)
    for k in range(2):
        found = []
        for e in range(2):
            rows = []
            for half in range(2):
                for c in range(2):
                    row = alm[e, c : c + 1, :]
                    rows.append(beam[k, 32 * half : 32 * half + 32, :] * row)
            product = jnp.concatenate(rows, axis=0)
            found.append(lax.dot_general(wig[e, k], product, NT, preferred_element_type=F32))
        one = found[0] * first
        two = found[1] * (1.0 / 32.0)
        keep[pl.ds(k * 1152 + g, 128, stride=9), :] = jnp.where(lane < 64, one, pltpu.roll(two, 64, 1))
        send[pl.ds(k * 1152 + g, 128, stride=9), :] = jnp.where(lane < 64, pltpu.roll(one, 64, 1), two)


def spectra_call(place, wig, alm, beam, crossing, offsets, fraction):
    whole = lambda shape: pl.BlockSpec(shape, lambda g, p: (0,) * len(shape))
    return pl.pallas_call(
        spectra_kernel,
        grid_spec=pltpu.PrefetchScalarGridSpec(
            num_scalar_prefetch=1,
            grid=(8,),
            in_specs=[
                pl.BlockSpec((2, 2, 128, 1024), lambda g, p: (g, 0, 0, 0)),
                pl.BlockSpec((2, 2, 1024), lambda g, p: (g, 0, p[0])),
                whole((2, 64, 1024)),
                whole((1, 128)),
                whole((32, 128)),
                whole((32, 128)),
            ],
            out_specs=[whole((2304, 128)), whole((2304, 128)), whole((1, 128))],
            scratch_shapes=[pltpu.VMEM((128, 128), F32)],
        ),
        out_shape=[
            jax.ShapeDtypeStruct((2304, 128), F32),
            jax.ShapeDtypeStruct((2304, 128), F32),
            jax.ShapeDtypeStruct((1, 128), I32),
        ],
        name="spectra",
    )(place, wig, alm, beam, crossing, offsets, fraction)


def tables():
    d = np.arange(128)[:, None]
    p = np.arange(256)[None, :]
    angle = 2.0 * np.pi * ((d * p) % 256) / 256.0
    cos, sin = np.cos(angle), np.sin(angle)
    dft = np.concatenate(
        [np.concatenate([cos, sin], axis=1), np.concatenate([-sin, cos], axis=1)], axis=0
    )
    hi = dft.astype(np.float32).astype(BF16)
    lo = (dft - hi.astype(np.float64)).astype(np.float32).astype(BF16)
    e = np.arange(16)[:, None]
    turn = 2.0 * np.pi * e * p / 4096.0
    return hi, lo, np.cos(turn).astype(np.float32), np.sin(turn).astype(np.float32)


def real_dft16(zr, zi):
    c = math.sqrt(0.5)
    c1, c3 = math.cos(math.pi / 8), math.cos(3 * math.pi / 8)
    s1, s3 = math.sin(math.pi / 8), math.sin(3 * math.pi / 8)
    a = [zr[0]] + [zr[e] + zr[16 - e] for e in range(1, 8)] + [zr[8]]
    b = [None] + [zi[e] - zi[16 - e] for e in range(1, 8)]
    p08, m08 = a[0] + a[8], a[0] - a[8]
    s26, d26 = a[2] + a[6], (a[2] - a[6]) * c
    s17, d17, s35, d35 = a[1] + a[7], a[1] - a[7], a[3] + a[5], a[3] - a[5]
    even = [p08 + a[4] + s26, m08 + d26, p08 - a[4], m08 - d26, p08 + a[4] - s26]
    odd = [s17 + s35, d17 * c1 + d35 * c3, (s17 - s35) * c, d17 * c3 - d35 * c1]
    cosine = [None] * 9
    for p in range(4):
        cosine[p] = even[p] + odd[p]
        cosine[8 - p] = even[p] - odd[p]
    cosine[4] = even[4]
    t17, u17, t35, u35 = b[1] + b[7], b[1] - b[7], b[3] + b[5], b[3] - b[5]
    t26, u26 = (b[2] + b[6]) * c, b[2] - b[6]
    bo = [None, t17 * s1 + t35 * s3, (u17 + u35) * c, t17 * s3 - t35 * s1]
    be = [None, t26 + b[4], u26, t26 - b[4]]
    sine = [None] * 8
    for p in range(1, 4):
        sine[p] = bo[p] + be[p]
        sine[8 - p] = bo[p] - be[p]
    sine[4] = u17 - u35
    out = [None] * 16
    out[0], out[8] = cosine[0], cosine[8]
    for p in range(1, 8):
        out[p] = cosine[p] - sine[p]
        out[16 - p] = cosine[p] + sine[p]
    return out


def lagrange_weights(position):
    shifted = position + 1.0
    minus_one = position - 1.0
    minus_two = position - 2.0
    return (
        -position * minus_one * minus_two / 6.0,
        shifted * minus_one * minus_two / 2.0,
        -shifted * position * minus_two / 2.0,
        shifted * position * minus_one / 6.0,
    )


def circle_kernel(
    got, hi, lo, tcos, tsin, out, wide, left, field, tiles, grid_o, grid_w, ids_v, ids_s, sem
):
    wide[...] = got[...].astype(F32)
    lane = lanes_of((128, 128))
    for s in range(2):
        flipped = jnp.transpose(wide[pl.ds(8 + 9 * s, 128, stride=18), :])
        ids_v[8 * s : 8 * s + 8, :] = flipped[96:104, :].astype(I32)
    copy = pltpu.make_async_copy(ids_v, ids_s, sem)
    copy.start()
    for i in range(2):
        for g in range(8):
            flipped = jnp.transpose(wide[pl.ds(9 * i + g, 128, stride=18), :]).astype(BF16)
            for e in range(2):
                base = (2 * g + e) * 64 + 32 * i
                left[base : base + 32, 0:128] = flipped[64 * e : 64 * e + 32]
                left[base : base + 32, 128:256] = flipped[64 * e + 32 : 64 * e + 64]
    field[...] = jnp.dot(left[...], hi[...], preferred_element_type=F32) + jnp.dot(
        left[...], lo[...], preferred_element_type=F32
    )
    for half in range(2):
        re = slice(128 * half, 128 * half + 128)
        im = slice(256 + 128 * half, 256 + 128 * half + 128)
        for r in range(4):
            zr, zi = [], []
            for e in range(16):
                yr = field[64 * e + 16 * r : 64 * e + 16 * r + 16, re]
                yi = field[64 * e + 16 * r : 64 * e + 16 * r + 16, im]
                tc, ts = tcos[e : e + 1, re], tsin[e : e + 1, re]
                zr.append(yr * tc - yi * ts)
                zi.append(yr * ts + yi * tc)
            i, j = r // 2, r % 2
            for p, x in enumerate(real_dft16(zr, zi)):
                tiles[32 * i + 2 * p + half, 16 * j : 16 * j + 16, :] = x.astype(BF16)
    part = lax.broadcasted_iota(I32, (64, 128), 1) // 32
    o = jnp.zeros((64, 128), F32)
    f = jnp.zeros((64, 128), F32)
    for n in range(2):
        for s in range(2):
            x = wide[pl.ds(18 * n + 8 + 9 * s, 64, stride=36), :]
            to = 2 * n + s
            o = jnp.where(part == to, pltpu.roll(x, 32 * to, 1), o)
            y = x + pltpu.roll(x, 96, 1)
            f = jnp.where(part == to, pltpu.roll(y, (32 * to + 96) % 128, 1), f)
    grid_o[...] = o
    for place, w in enumerate(lagrange_weights(f)):
        grid_w[place] = w
    copy.wait()
    sub = lax.broadcasted_iota(I32, (128, 128), 0).astype(F32)
    lane32 = lanes_of((32, 128)) // 32
    lane16 = lanes_of((16, 128))

    def pair(t, carry):
        distance = sub - grid_o[pl.ds(t, 1), :]
        matrix = jnp.zeros((128, 128), F32)
        for place in range(4):
            matrix = jnp.where(distance == place, grid_w[place, pl.ds(t, 1), :], matrix)
        stack = jnp.concatenate(
            [tiles[ids_s[8 * s, 2 * t + n]] for n in range(2) for s in range(2)], axis=0
        )
        res = jnp.dot(stack, matrix.astype(BF16), preferred_element_type=F32)
        d = res[0:32]
        for q in range(1, 4):
            d = jnp.where(lane32 == q, res[32 * q : 32 * q + 32], d)
        a, b = d[0:16], d[16:32]
        row = pl.multiple_of(t * 32, 32)
        out[pl.ds(row, 16), :] = jnp.where(lane16 < 64, a, pltpu.roll(b, 64, 1)).astype(BF16)
        out[pl.ds(row + 16, 16), :] = jnp.where(lane16 < 64, pltpu.roll(a, 64, 1), b).astype(BF16)
        return carry

    lax.fori_loop(0, 64, pair, 0, unroll=2)


def circle_call(got):
    hi, lo, tcos, tsin = tables()
    vmem = pl.BlockSpec(memory_space=pltpu.VMEM)
    return pl.pallas_call(
        circle_kernel,
        in_specs=[vmem] * 5,
        out_specs=vmem,
        out_shape=jax.ShapeDtypeStruct((2048, 128), BF16),
        scratch_shapes=[
            pltpu.VMEM((2304, 128), F32),
            pltpu.VMEM((1024, 256), BF16),
            pltpu.VMEM((1024, 512), F32),
            pltpu.VMEM((64, 32, 128), BF16),
            pltpu.VMEM((64, 128), F32),
            pltpu.VMEM((4, 64, 128), F32),
            pltpu.VMEM((16, 128), I32),
            pltpu.SMEM((16, 128), I32),
            pltpu.SemaphoreType.DMA,
        ],
        name="circle",
    )(got, jnp.asarray(hi), jnp.asarray(lo), jnp.asarray(tcos), jnp.asarray(tsin))


def circulant(v):
    x = jnp.broadcast_to(v, (128, 128))
    sub = lax.broadcasted_iota(I32, (128, 128), 0)
    for bit in range(7):
        x = jnp.where((lax.shift_right_logical(sub, bit) & 1) == 1, pltpu.roll(x, 1 << bit, 1), x)
    return x


def two_parts(x):
    hi = x.astype(BF16)
    return hi, (x - hi.astype(F32)).astype(BF16)


def ends_kernel(flat, last, head, out):
    lane = lanes_of((32, 128))
    for which, (ref, q, to) in enumerate(((last, 127, 96), (head, 0, 0))):
        slot = flat[q] & 1
        x = ref[...].astype(F32)
        shift = to - 32 * slot + 128
        both = jnp.concatenate(
            [pltpu.roll(x, lax.rem(shift, 128), 1), pltpu.roll(x, lax.rem(shift + 64, 128), 1)], axis=0
        )
        out[which] = jnp.where((lane >= to) & (lane < to + 32), both, 0.0).astype(BF16)


def ends_call(flat, came):
    return pl.pallas_call(
        ends_kernel,
        grid_spec=pltpu.PrefetchScalarGridSpec(
            num_scalar_prefetch=1,
            grid=(1,),
            in_specs=[
                pl.BlockSpec((16, 128), lambda i, f: (lax.shift_right_logical(f[127], 1), 0)),
                pl.BlockSpec((16, 128), lambda i, f: (lax.shift_right_logical(f[0], 1), 0)),
            ],
            out_specs=pl.BlockSpec((2, 32, 128), lambda i, f: (0, 0, 0)),
        ),
        out_shape=jax.ShapeDtypeStruct((2, 32, 128), BF16),
        name="ends",
    )(flat, came, came)


def signal_kernel(flat, came, v, out, line):
    lane = lanes_of((16, 128)) // 32
    line[1, :, 0:128] = jnp.zeros((32, 128), BF16)
    line[32, :, 256:384] = jnp.zeros((32, 128), BF16)

    def block(b, carry):
        low = jnp.zeros((16, 128), F32)
        high = jnp.zeros((16, 128), F32)
        for q in range(4):
            at = flat[4 * b + q]
            row = pl.multiple_of(lax.shift_right_logical(at, 1) * 16, 16)
            x = came[pl.ds(row, 16), :].astype(F32)
            shift = 32 * q + 128 - 32 * (at & 1)
            low = jnp.where(lane == q, pltpu.roll(x, lax.rem(shift, 128), 1), low)
            high = jnp.where(lane == q, pltpu.roll(x, lax.rem(shift + 64, 128), 1), high)
        x = jnp.concatenate([low, high], axis=0).astype(BF16)
        line[b + 1, :, 128:256] = x
        line[b + 2, :, 0:128] = x
        line[b, :, 256:384] = x
        return carry

    lax.fori_loop(0, 32, block, 0, unroll=2)
    ring = circulant(v[...])
    sub = lax.broadcasted_iota(I32, (128, 128), 0)
    gap = lanes_of((128, 128)) - sub
    band = jnp.concatenate(
        [
            jnp.where(gap < -64, ring, 0.0),
            jnp.where((gap >= -64) & (gap <= 64), ring, 0.0),
            jnp.where(gap > 64, ring, 0.0),
        ],
        axis=0,
    )
    hi, lo = two_parts(band)
    for b in range(0, 32, 4):
        x = line[b + 1 : b + 5].reshape(128, 384)
        y = jnp.dot(x, hi, preferred_element_type=F32) + jnp.dot(x, lo, preferred_element_type=F32)
        for i in range(4):
            out[:, 128 * (b + i) : 128 * (b + i) + 128] = y[32 * i : 32 * i + 32]


def signal_call(flat, came, v):
    whole = lambda shape: pl.BlockSpec(shape, lambda i, f: (0,) * len(shape))
    return pl.pallas_call(
        signal_kernel,
        grid_spec=pltpu.PrefetchScalarGridSpec(
            num_scalar_prefetch=1,
            grid=(1,),
            in_specs=[whole((2048, 128)), whole((1, 128))],
            out_specs=whole((32, 4096)),
            scratch_shapes=[pltpu.VMEM((34, 32, 384), BF16)],
        ),
        out_shape=jax.ShapeDtypeStruct((32, 4096), F32),
        cost_estimate=pl.CostEstimate(flops=400_000_000, bytes_accessed=4_000_000, transcendentals=0),
        name="signal",
    )(flat, came, v)


def edge_kernel(y, before, after, v, out):
    ring = circulant(v[...])
    gap = lanes_of((128, 128)) - lax.broadcasted_iota(I32, (128, 128), 0)

    def add(x, mask):
        hi, lo = two_parts(jnp.where(mask, ring, 0.0))
        out[...] = (
            y[...] + jnp.dot(x, hi, preferred_element_type=F32) + jnp.dot(x, lo, preferred_element_type=F32)
        )

    @pl.when(pl.program_id(0) == 0)
    def first():
        add(before[...], gap < -64)

    @pl.when(pl.program_id(0) == 1)
    def last():
        add(after[...], gap > 64)


def edge_call(y, before, after, v):
    whole = lambda shape: pl.BlockSpec(shape, lambda i: (0,) * len(shape))
    block = pl.BlockSpec((32, 128), lambda i: (0, 31 * i))
    return pl.pallas_call(
        edge_kernel,
        grid=(2,),
        in_specs=[block, whole((32, 128)), whole((32, 128)), whole((1, 128))],
        out_specs=block,
        out_shape=jax.ShapeDtypeStruct((32, 4096), F32),
        input_output_aliases={0: 0},
        name="edge",
    )(y, before, after, v)


def local(wigner, alm, beam, crossing, offsets, fraction, taps):
    det = lax.axis_index("det")
    half = wigner.shape[3]
    place = jnp.stack([det, lax.axis_index("ord")]).astype(I32)
    mine = lax.dynamic_slice(beam, (det * DET, 0, det * half), (DET, 2, half))
    other = lax.dynamic_slice(beam, ((1 - det) * DET, 0, det * half), (DET, 2, half))
    beams = jnp.transpose(jnp.concatenate([mine, other], axis=0), (1, 0, 2))
    keep, send, flat = spectra_call(
        place, wigner, alm, beams, crossing, offsets.reshape(32, 128), fraction.reshape(32, 128)
    )
    partner = lax.ppermute(send, "det", [(0, 1), (1, 0)])
    message = (keep + partner).astype(BF16).reshape(ORD, ROWS, 2, 128)
    arrived = lax.all_to_all(message, "ord", split_axis=0, concat_axis=0, tiled=True)
    outgoing = circle_call(arrived.reshape(ORD * 2 * ROWS, 128))
    came = lax.all_to_all(
        outgoing.reshape(ORD, 16, 128), "ord", split_axis=0, concat_axis=0, tiled=True
    ).reshape(2048, 128)
    slots = flat.reshape(128)
    ends = ends_call(slots, came)
    before = lax.ppermute(ends[0], "ord", [(i, i + 1) for i in range(ORD - 1)])
    after = lax.ppermute(ends[1], "ord", [(i + 1, i) for i in range(ORD - 1)])
    v = jnp.concatenate([taps[16::-1], jnp.zeros((95,), F32), taps[:16:-1]]).reshape(1, 128)
    return edge_call(signal_call(slots, came, v), before, after, v)


def solution(mesh):
    return jax.shard_map(
        local,
        mesh=mesh,
        in_specs=(
            P("ord", None, None, "det"),
            P("ord", None, None),
            P(),
            P("ord", None),
            P("ord", None),
            P("ord", None),
            P(),
        ),
        out_specs=P("det", "ord"),
        check_vma=False,
    )
```

```python
import math

import jax
import jax.numpy as jnp
import numpy as np
from jax import lax
from jax.experimental import pallas as pl
from jax.experimental.pallas import tpu as pltpu
from jax.sharding import PartitionSpec as P

F32 = jnp.float32
BF16 = jnp.bfloat16
I32 = jnp.int32

ORD = 128
ROWS = 9
NT = (((1,), (1,)), ((), ()))


def lanes_of(shape):
    return lax.broadcasted_iota(I32, shape, len(shape) - 1)


def spectra_kernel(
    det_ref, ord_ref, wig, alm, beam, crossing, offsets, fraction, keep, send, flat, cells, wide, beams, product, found
):
    g = pl.program_id(0)
    det = det_ref[0]

    def build(slot, k, m):
        for half in range(2):
            for c in range(2):
                row = alm[m, c : c + 1, :]
                at = 64 * half + 32 * c
                product[slot, at : at + 32, :] = beams[k, 32 * half : 32 * half + 32, :] * row

    @pl.when(g == 0)
    def prepare():
        wide[...] = beam[:, pl.ds(pl.multiple_of(16 * det, 16), 16), :].astype(F32).reshape(1024, 128)
        for half in range(2):
            base = (32 * det if half == 0 else 32 * (1 - det)) * 16
            for k in range(2):
                for t in range(8):
                    x = wide[pl.ds(base + 2 * t + k, 32, stride=16), :]
                    beams[k, 32 * half : 32 * half + 32, 128 * t : 128 * t + 128] = x.astype(BF16)
        build(0, 0, 0)
        c = crossing[...]
        holder = lax.shift_right_logical(c, 6)
        across = jnp.broadcast_to(holder, (128, 128)).astype(F32)
        down = jnp.transpose(across)
        sub = lax.broadcasted_iota(I32, (128, 128), 0)
        lane = lanes_of((128, 128))
        earlier = jnp.where((across == down) & (sub < lane), 1.0, 0.0)
        slot = jnp.sum(earlier, axis=0, keepdims=True).astype(I32)
        flat[...] = holder * 2 + slot
        o32 = offsets[...].astype(F32)
        f32_ = fraction[...]
        hi = f32_.astype(BF16).astype(F32)
        lo = f32_ - hi
        lane32 = lanes_of((32, 128))
        ids = jnp.broadcast_to((c & 63).astype(F32), (128, 128))
        ids = jnp.sum(jnp.where(sub == lane, ids, 0.0), axis=1, keepdims=True)
        end = ((lane < 112) & (sub == 0)) | ((lane >= 112) & (sub == 127))
        ids = jnp.broadcast_to(ids, (128, 128)) + jnp.where(end, 64.0, 0.0)
        for part in range(4):
            sh = 128 - 32 * part
            row = jnp.where(
                lane32 < 32,
                pltpu.roll(o32, sh % 128, 1),
                jnp.where(
                    lane32 < 64, pltpu.roll(hi, (sh + 32) % 128, 1), pltpu.roll(lo, (sh + 64) % 128, 1)
                ),
            )
            cells[pl.ds(part, 32, stride=4), :] = row
        data = jnp.where(lane < 96, cells[...], ids).astype(BF16)
        for s in range(2):
            pick = jnp.where((sub == holder) & (slot == s), 1.0, 0.0).astype(BF16)
            got = jnp.dot(pick, data, preferred_element_type=F32)
            keep[pl.ds(8 + 9 * s, 128, stride=18), :] = got
            send[pl.ds(8 + 9 * s, 128, stride=18), :] = jnp.zeros((128, 128), F32)

    lane = lanes_of((128, 128))

    def place(step):
        first = jnp.where((ord_ref[0] == 0) & (step == 0), 1.0 / 64.0, 1.0 / 32.0)
        for k in range(2):
            one = found[2 * k] * first
            two = found[2 * k + 1] * (1.0 / 32.0)
            row = pl.ds(k * 1152 + step, 128, stride=9)
            keep[row, :] = jnp.where(lane < 64, one, pltpu.roll(two, 64, 1))
            send[row, :] = jnp.where(lane < 64, pltpu.roll(one, 64, 1), two)

    place(jnp.maximum(g - 1, 0))
    for unit in range(4):
        k, e = unit // 2, unit % 2
        following = jnp.minimum(2 * g + 2, 15) if unit == 3 else 2 * g + 1 - e
        build((unit + 1) % 2, (unit + 1) // 2 % 2, following)
        found[unit] = lax.dot_general(wig[e, k], product[unit % 2], NT, preferred_element_type=F32)

    @pl.when(g == 7)
    def last():
        place(7)


def spectra_call(det, order, wig, alm, beam, crossing, offsets, fraction):
    whole = lambda shape: pl.BlockSpec(shape, lambda g, d, o: (0,) * len(shape))
    return pl.pallas_call(
        spectra_kernel,
        grid_spec=pltpu.PrefetchScalarGridSpec(
            num_scalar_prefetch=2,
            grid=(8,),
            in_specs=[
                pl.BlockSpec((2, 2, 128, 1024), lambda g, d, o: (g, 0, 0, 0)),
                pl.BlockSpec((16, 2, 1024), lambda g, d, o: (0, 0, d[0])),
                whole((64, 32, 128)),
                whole((1, 128)),
                whole((32, 128)),
                whole((32, 128)),
            ],
            out_specs=[whole((2304, 128)), whole((2304, 128)), whole((1, 128))],
            scratch_shapes=[
                pltpu.VMEM((128, 128), F32),
                pltpu.VMEM((1024, 128), F32),
                pltpu.VMEM((2, 64, 1024), BF16),
                pltpu.VMEM((2, 128, 1024), BF16),
                pltpu.VMEM((4, 128, 128), F32),
            ],
        ),
        out_shape=[
            jax.ShapeDtypeStruct((2304, 128), F32),
            jax.ShapeDtypeStruct((2304, 128), F32),
            jax.ShapeDtypeStruct((1, 128), I32),
        ],
        name="spectra",
    )(det, order, wig, alm, beam, crossing, offsets, fraction)


def tables():
    d = np.arange(128)[:, None]
    p = np.arange(256)[None, :]
    here = 2.0 * np.pi * ((d * p) % 256) / 256.0
    after = 2.0 * np.pi * (((d + 1) * p) % 256) / 256.0
    eighth = here + 2.0 * np.pi * 8 * p / 4096.0
    cat = np.concatenate
    real = cat([np.cos(here), -np.sin(here), np.cos(after), -np.sin(after)], axis=0)
    imag = cat([np.sin(here), np.cos(here), -np.sin(after), -np.cos(after)], axis=0)
    folded = cat([real, imag], axis=1)
    ends = cat([cat([np.cos(x), -np.sin(x)], axis=0) for x in (here, eighth)], axis=1)
    turn = 2.0 * np.pi * np.arange(8)[:, None] * p / 4096.0
    small = lambda x: x.astype(np.float32).astype(BF16)
    return small(folded), small(ends), np.cos(turn).astype(np.float32), np.sin(turn).astype(np.float32)


def real_dft16(a, b):
    c = math.sqrt(0.5)
    c1, c3 = math.cos(math.pi / 8), math.cos(3 * math.pi / 8)
    s1, s3 = math.sin(math.pi / 8), math.sin(3 * math.pi / 8)
    p08, m08 = a[0] + a[8], a[0] - a[8]
    s26, d26 = a[2] + a[6], (a[2] - a[6]) * c
    s17, d17, s35, d35 = a[1] + a[7], a[1] - a[7], a[3] + a[5], a[3] - a[5]
    even = [p08 + a[4] + s26, m08 + d26, p08 - a[4], m08 - d26, p08 + a[4] - s26]
    odd = [s17 + s35, d17 * c1 + d35 * c3, (s17 - s35) * c, d17 * c3 - d35 * c1]
    cosine = [None] * 9
    for p in range(4):
        cosine[p] = even[p] + odd[p]
        cosine[8 - p] = even[p] - odd[p]
    cosine[4] = even[4]
    t17, u17, t35, u35 = b[1] + b[7], b[1] - b[7], b[3] + b[5], b[3] - b[5]
    t26, u26 = (b[2] + b[6]) * c, b[2] - b[6]
    bo = [None, t17 * s1 + t35 * s3, (u17 + u35) * c, t17 * s3 - t35 * s1]
    be = [None, t26 + b[4], u26, t26 - b[4]]
    sine = [None] * 8
    for p in range(1, 4):
        sine[p] = bo[p] + be[p]
        sine[8 - p] = bo[p] - be[p]
    sine[4] = u17 - u35
    out = [None] * 16
    out[0], out[8] = cosine[0], cosine[8]
    for p in range(1, 8):
        out[p] = cosine[p] - sine[p]
        out[16 - p] = cosine[p] + sine[p]
    return out


def lagrange_weights(position):
    shifted = position + 1.0
    minus_one = position - 1.0
    minus_two = position - 2.0
    return (
        -position * minus_one * minus_two / 6.0,
        shifted * minus_one * minus_two / 2.0,
        -shifted * position * minus_two / 2.0,
        shifted * position * minus_one / 6.0,
    )


def circle_kernel(
    got, folded, single, tcos, tsin, out,
    wide, left, left0, left8, field, field0, field8, tiles, grid_o, grid_w, ends, mark, ids_v, ids_s, sem,
):
    wide[...] = got[...].astype(F32)
    for s in range(2):
        flipped = jnp.transpose(wide[pl.ds(8 + 9 * s, 128, stride=18), :])
        ids_v[8 * s : 8 * s + 8, :] = flipped[96:104, :].astype(I32) & 63
    copy = pltpu.make_async_copy(ids_v, ids_s, sem)
    copy.start()
    for i in range(2):
        for g in range(8):
            flipped = jnp.transpose(wide[pl.ds(9 * i + g, 128, stride=18), :]).astype(BF16)
            for odd in range(2):
                e = 2 * g + odd
                if e % 8 == 0:
                    to, row, lane0 = (left0 if e == 0 else left8), 32 * i, 0
                else:
                    to, row, lane0 = left, (min(e, 16 - e) - 1) * 64 + 32 * i, 0 if e < 8 else 256
                to[row : row + 32, lane0 : lane0 + 128] = flipped[64 * odd : 64 * odd + 32]
                to[row : row + 32, lane0 + 128 : lane0 + 256] = flipped[64 * odd + 32 : 64 * odd + 64]
    field[...] = jnp.dot(left[...], folded[...], preferred_element_type=F32)
    field0[...] = jnp.dot(left0[...], single[:, 0:256], preferred_element_type=F32)
    field8[...] = jnp.dot(left8[...], single[:, 256:512], preferred_element_type=F32)
    for half in range(2):
        re = slice(128 * half, 128 * half + 128)
        im = slice(256 + 128 * half, 256 + 128 * half + 128)
        for r in range(4):
            a, b = [field0[16 * r : 16 * r + 16, re]], [None]
            for e in range(1, 8):
                row = slice(64 * (e - 1) + 16 * r, 64 * (e - 1) + 16 * r + 16)
                yr, yi = field[row, re], field[row, im]
                tc, ts = tcos[e : e + 1, re], tsin[e : e + 1, re]
                a.append(yr * tc - yi * ts)
                b.append(yr * ts + yi * tc)
            a.append(field8[16 * r : 16 * r + 16, re])
            i, j = r // 2, r % 2
            for p, x in enumerate(real_dft16(a, b)):
                tiles[32 * i + 2 * p + half, 16 * j : 16 * j + 16, :] = x.astype(BF16)
    part = lanes_of((64, 128)) // 32
    o = jnp.zeros((64, 128), F32)
    f = jnp.zeros((64, 128), F32)
    for n in range(2):
        for s in range(2):
            x = wide[pl.ds(18 * n + 8 + 9 * s, 64, stride=36), :]
            to = 2 * n + s
            o = jnp.where(part == to, pltpu.roll(x, 32 * to, 1), o)
            y = x + pltpu.roll(x, 96, 1)
            f = jnp.where(part == to, pltpu.roll(y, (32 * to + 96) % 128, 1), f)
    grid_o[...] = o
    for place, w in enumerate(lagrange_weights(f)):
        grid_w[place] = w
    part = lanes_of((128, 128)) // 32
    one = wide[pl.ds(8, 128, stride=18), :]
    two = wide[pl.ds(17, 128, stride=18), :]
    mark[...] = jnp.where(
        part < 2,
        jnp.where(part == 0, pltpu.roll(one, 32, 1), pltpu.roll(two, 64, 1)),
        jnp.where(part == 2, pltpu.roll(one, 96, 1), two),
    )
    ends[0] = jnp.zeros((8, 128), F32)
    ends[129] = jnp.zeros((8, 128), F32)
    copy.wait()
    sub = lax.broadcasted_iota(I32, (128, 128), 0).astype(F32).astype(BF16)
    lane32 = lanes_of((32, 128)) // 32
    low16 = lanes_of((16, 128)) < 64
    even8 = (lanes_of((8, 128)) // 32) % 2 == 0

    def pair(t, carry):
        row = lambda ref: jnp.broadcast_to(ref[pl.ds(t, 1), :], (128, 128)).astype(BF16)
        distance = sub - row(grid_o)
        matrix = jnp.zeros((128, 128), BF16)
        for place in range(4):
            matrix = jnp.where(distance == place, row(grid_w.at[place]), matrix)
        stack = jnp.concatenate(
            [tiles[ids_s[8 * s, 2 * t + n]] for n in range(2) for s in range(2)], axis=0
        )
        res = jnp.dot(stack, matrix, preferred_element_type=F32)
        d = res[0:32]
        for q in range(1, 4):
            d = jnp.where(lane32 == q, res[32 * q : 32 * q + 32], d)
        a, b = d[0:16], d[16:32]
        for n in range(2):
            m = 2 * t + n
            x = jnp.where(low16, a, pltpu.roll(b, 64, 1)) if n == 0 else jnp.where(low16, pltpu.roll(a, 64, 1), b)
            out[m, 0:16, :] = x.astype(BF16)
            x = jnp.where(mark[pl.ds(m, 1), :] >= 64.0, x, 0.0)
            x = x + pltpu.roll(x, 96, 1)
            ends[m + 1] = jnp.where(even8, x[0:8], pltpu.roll(x[8:16], 32, 1))
        return carry

    lax.fori_loop(0, 64, pair, 0, unroll=4)
    tail = lanes_of((8, 128)) % 32 >= 16

    def rims(n, carry):
        out[n, 16:24, :] = jnp.where(tail, ends[n], ends[n + 2]).astype(BF16)
        return carry

    lax.fori_loop(0, 128, rims, 0, unroll=16)


def circle_call(got):
    folded, single, tcos, tsin = tables()
    vmem = pl.BlockSpec(memory_space=pltpu.VMEM)
    return pl.pallas_call(
        circle_kernel,
        in_specs=[vmem] * 5,
        out_specs=vmem,
        out_shape=jax.ShapeDtypeStruct((128, 24, 128), BF16),
        scratch_shapes=[
            pltpu.VMEM((2304, 128), F32),
            pltpu.VMEM((448, 512), BF16),
            pltpu.VMEM((64, 256), BF16),
            pltpu.VMEM((64, 256), BF16),
            pltpu.VMEM((448, 512), F32),
            pltpu.VMEM((64, 256), F32),
            pltpu.VMEM((64, 256), F32),
            pltpu.VMEM((64, 32, 128), BF16),
            pltpu.VMEM((64, 128), F32),
            pltpu.VMEM((4, 64, 128), F32),
            pltpu.VMEM((130, 8, 128), F32),
            pltpu.VMEM((128, 128), F32),
            pltpu.VMEM((16, 128), I32),
            pltpu.SMEM((16, 128), I32),
            pltpu.SemaphoreType.DMA,
        ],
        name="circle",
    )(got, *map(jnp.asarray, (folded, single, tcos, tsin)))


def circulant(v):
    x = jnp.broadcast_to(v, (128, 128))
    sub = lax.broadcasted_iota(I32, (128, 128), 0)
    for bit in range(7):
        x = jnp.where((lax.shift_right_logical(sub, bit) & 1) == 1, pltpu.roll(x, 1 << bit, 1), x)
    return x


def two_parts(x):
    hi = x.astype(BF16)
    return hi, (x - hi.astype(F32)).astype(BF16)


def signal_kernel(flat, came, v, out, line, result):
    lane = lanes_of((16, 128)) // 32
    lane32 = lanes_of((32, 128))

    def add(h, total):
        return total + came[h, 16:24, :].astype(F32)

    total = lax.fori_loop(0, 128, add, jnp.zeros((8, 128), F32), unroll=16)
    rim = jnp.concatenate([total] + [pltpu.roll(total, 128 - 32 * j, 1) for j in range(1, 4)], axis=0)
    before = pltpu.roll(rim, 96, 1).astype(BF16)
    after = rim.astype(BF16)

    def block(b, carry):
        older, newer = carry
        low = jnp.zeros((16, 128), F32)
        high = jnp.zeros((16, 128), F32)
        for q in range(4):
            at = flat[4 * b + q]
            x = came[lax.shift_right_logical(at, 1), 0:16, :].astype(F32)
            shift = 32 * q + 128 - 32 * (at & 1)
            low = jnp.where(lane == q, pltpu.roll(x, lax.rem(shift, 128), 1), low)
            high = jnp.where(lane == q, pltpu.roll(x, lax.rem(shift + 64, 128), 1), high)
        x = jnp.concatenate([low, high], axis=0).astype(BF16)
        line[b + 1, :, 0:128] = x
        line[b, :, 128:256] = jnp.where(lane32 < 64, x, older)
        return newer, x

    older, newer = lax.fori_loop(0, 32, block, (jnp.zeros((32, 128), BF16), before), unroll=4)
    line[32, :, 128:256] = jnp.where(lane32 < 64, after, older)
    ring = circulant(v[...])
    gap = lanes_of((128, 128)) - lax.broadcasted_iota(I32, (128, 128), 0)
    near = (gap >= -64) & (gap <= 64)
    hi, lo = two_parts(jnp.concatenate([jnp.where(near, ring, 0.0), jnp.where(near, 0.0, ring)], axis=0))
    result[...] = jnp.dot(
        line[1:33].reshape(1024, 256), jnp.concatenate([hi, lo], axis=1), preferred_element_type=F32
    )
    for b in range(32):
        y = result[32 * b : 32 * b + 32, :]
        out[:, 128 * b : 128 * b + 128] = y[:, 0:128] + y[:, 128:256]


def signal_call(flat, came, v):
    whole = lambda shape: pl.BlockSpec(shape, lambda i, f: (0,) * len(shape))
    return pl.pallas_call(
        signal_kernel,
        grid_spec=pltpu.PrefetchScalarGridSpec(
            num_scalar_prefetch=1,
            grid=(1,),
            in_specs=[whole((128, 24, 128)), whole((1, 128))],
            out_specs=whole((32, 4096)),
            scratch_shapes=[pltpu.VMEM((33, 32, 256), BF16), pltpu.VMEM((1024, 256), F32)],
        ),
        out_shape=jax.ShapeDtypeStruct((32, 4096), F32),
        name="signal",
    )(flat, came, v)


def local(wigner, alm, beam, crossing, offsets, fraction, taps):
    det = lax.axis_index("det").astype(I32).reshape(1)
    order = lax.axis_index("ord").astype(I32).reshape(1)
    beams = beam.reshape(64, 2, 16, 128).transpose(0, 2, 1, 3).reshape(64, 32, 128)
    keep, send, flat = spectra_call(
        det, order, wigner, alm, beams, crossing, offsets.reshape(32, 128), fraction.reshape(32, 128)
    )
    partner = lax.ppermute(send, "det", [(0, 1), (1, 0)])
    message = (keep + partner).astype(BF16).reshape(ORD, ROWS, 2, 128)
    arrived = lax.all_to_all(message, "ord", split_axis=0, concat_axis=0, tiled=True)
    outgoing = circle_call(arrived.reshape(ORD * 2 * ROWS, 128))
    came = lax.all_to_all(outgoing, "ord", split_axis=0, concat_axis=0, tiled=True)
    v = jnp.concatenate([taps[16::-1], jnp.zeros((95,), F32), taps[:16:-1]]).reshape(1, 128)
    return signal_call(flat.reshape(128), came, v)


def solution(mesh):
    return jax.shard_map(
        local,
        mesh=mesh,
        in_specs=(
            P("ord", None, None, "det"),
            P("ord", None, None),
            P(),
            P("ord", None),
            P("ord", None),
            P("ord", None),
            P(),
        ),
        out_specs=P("det", "ord"),
        check_vma=False,
    )
```

```python
import math

import jax
import jax.numpy as jnp
import numpy as np
from jax import lax
from jax.experimental import pallas as pl
from jax.experimental.pallas import tpu as pltpu
from jax.sharding import PartitionSpec as P

F32 = jnp.float32
BF16 = jnp.bfloat16
I32 = jnp.int32

ORD = 128
ROWS = 9
NT = (((1,), (1,)), ((), ()))


def lanes_of(shape):
    return lax.broadcasted_iota(I32, shape, len(shape) - 1)


def near(x):
    return pltpu.with_memory_space_constraint(x, pltpu.VMEM)


def spectra_kernel(
    det_ref, ord_ref, wig_hbm, alm_hbm, beam_hbm, cross_hbm, offset_hbm, fraction_hbm, keep, send, flat,
    wig, alm, beam, crossing, offsets, fraction, cells, wide, beams, product, found, sems,
):
    det = det_ref[0]
    half_lanes = pl.ds(pl.multiple_of(1024 * det, 1024), 1024)
    copies = [
        pltpu.make_async_copy(beam_hbm.at[:, pl.ds(pl.multiple_of(16 * det, 16), 16), :], beam, sems.at[8]),
        pltpu.make_async_copy(cross_hbm, crossing, sems.at[9]),
        pltpu.make_async_copy(offset_hbm, offsets, sems.at[10]),
        pltpu.make_async_copy(fraction_hbm, fraction, sems.at[11]),
        pltpu.make_async_copy(alm_hbm.at[:, :, half_lanes], alm, sems.at[12]),
    ]
    block = lambda g: pltpu.make_async_copy(wig_hbm.at[pl.ds(2 * g, 2)], wig.at[pl.ds(2 * g, 2)], sems.at[g])
    for copy in copies:
        copy.start()
    for g in range(8):
        block(g).start()

    def build(slot, k, m):
        for half in range(2):
            for c in range(2):
                row = alm[m, c : c + 1, :]
                at = 64 * half + 32 * c
                product[slot, at : at + 32, :] = beams[k, 32 * half : 32 * half + 32, :] * row

    def prepare():
        copies[0].wait()
        wide[...] = beam[...].astype(F32).reshape(1024, 128)
        for half in range(2):
            base = (32 * det if half == 0 else 32 * (1 - det)) * 16
            for k in range(2):
                for t in range(8):
                    x = wide[pl.ds(base + 2 * t + k, 32, stride=16), :]
                    beams[k, 32 * half : 32 * half + 32, 128 * t : 128 * t + 128] = x.astype(BF16)
        for copy in copies[1:4]:
            copy.wait()
        c = crossing[...]
        holder = lax.shift_right_logical(c, 6)
        across = jnp.broadcast_to(holder, (128, 128)).astype(F32)
        down = jnp.transpose(across)
        sub = lax.broadcasted_iota(I32, (128, 128), 0)
        lane = lanes_of((128, 128))
        earlier = jnp.where((across == down) & (sub < lane), 1.0, 0.0)
        slot = jnp.sum(earlier, axis=0, keepdims=True).astype(I32)
        flat[...] = holder * 2 + slot
        o32 = offsets[...].astype(F32)
        f32_ = fraction[...]
        hi = f32_.astype(BF16).astype(F32)
        lo = f32_ - hi
        lane32 = lanes_of((32, 128))
        ids = jnp.broadcast_to((c & 63).astype(F32), (128, 128))
        ids = jnp.sum(jnp.where(sub == lane, ids, 0.0), axis=1, keepdims=True)
        end = ((lane < 112) & (sub == 0)) | ((lane >= 112) & (sub == 127))
        ids = jnp.broadcast_to(ids, (128, 128)) + jnp.where(end, 64.0, 0.0)
        for part in range(4):
            sh = 128 - 32 * part
            row = jnp.where(
                lane32 < 32,
                pltpu.roll(o32, sh % 128, 1),
                jnp.where(
                    lane32 < 64, pltpu.roll(hi, (sh + 32) % 128, 1), pltpu.roll(lo, (sh + 64) % 128, 1)
                ),
            )
            cells[pl.ds(part, 32, stride=4), :] = row
        data = jnp.where(lane < 96, cells[...], ids).astype(BF16)
        for s in range(2):
            pick = jnp.where((sub == holder) & (slot == s), 1.0, 0.0).astype(BF16)
            got = jnp.dot(pick, data, preferred_element_type=F32)
            keep[pl.ds(8 + 9 * s, 128, stride=18), :] = got
            send[pl.ds(8 + 9 * s, 128, stride=18), :] = jnp.zeros((128, 128), F32)

    lane = lanes_of((128, 128))

    def place(step):
        first = jnp.where((ord_ref[0] == 0) & (step == 0), 1.0 / 64.0, 1.0 / 32.0)
        for k in range(2):
            one = found[2 * k] * first
            two = found[2 * k + 1] * (1.0 / 32.0)
            row = pl.ds(k * 1152 + step, 128, stride=9)
            keep[row, :] = jnp.where(lane < 64, one, pltpu.roll(two, 64, 1))
            send[row, :] = jnp.where(lane < 64, pltpu.roll(one, 64, 1), two)

    prepare()
    copies[4].wait()

    def step(g, carry):
        block(g).wait()
        place(jnp.maximum(g - 1, 0))
        for unit in range(4):
            k, e = unit // 2, unit % 2
            build(unit, k, 2 * g + e)
            found[unit] = lax.dot_general(wig[2 * g + e, k], product[unit], NT, preferred_element_type=F32)
        return carry

    lax.fori_loop(0, 8, step, 0)
    place(7)


def spectra_call(det, order, wig, alm, beam, crossing, offsets, fraction):
    smem = pl.BlockSpec(memory_space=pltpu.SMEM)
    vmem = pl.BlockSpec(memory_space=pltpu.VMEM)
    return pl.pallas_call(
        spectra_kernel,
        in_specs=[smem, smem] + [pl.BlockSpec(memory_space=pl.ANY)] * 6,
        out_specs=[vmem] * 3,
        out_shape=[pltpu.VMEM((2304, 128), F32), pltpu.VMEM((2304, 128), F32), jax.ShapeDtypeStruct((1, 128), I32)],
        scratch_shapes=[
            pltpu.VMEM((16, 2, 128, 1024), BF16),
            pltpu.VMEM((16, 2, 1024), BF16),
            pltpu.VMEM((64, 16, 128), BF16),
            pltpu.VMEM((1, 128), I32),
            pltpu.VMEM((32, 128), I32),
            pltpu.VMEM((32, 128), F32),
            pltpu.VMEM((128, 128), F32),
            pltpu.VMEM((1024, 128), F32),
            pltpu.VMEM((2, 64, 1024), BF16),
            pltpu.VMEM((4, 128, 1024), BF16),
            pltpu.VMEM((4, 128, 128), F32),
            pltpu.SemaphoreType.DMA((13,)),
        ],
        name="spectra",
    )(det, order, wig, alm, beam, crossing, offsets, fraction)


def tables():
    d = np.arange(128)[:, None]
    p = np.arange(256)[None, :]
    here = 2.0 * np.pi * ((d * p) % 256) / 256.0
    after = 2.0 * np.pi * (((d + 1) * p) % 256) / 256.0
    eighth = here + 2.0 * np.pi * 8 * p / 4096.0
    cat = np.concatenate
    real = cat([np.cos(here), -np.sin(here), np.cos(after), -np.sin(after)], axis=0)
    imag = cat([np.sin(here), np.cos(here), -np.sin(after), -np.cos(after)], axis=0)
    folded = cat([real, imag], axis=1)
    ends = cat([cat([np.cos(x), -np.sin(x)], axis=0) for x in (here, eighth)], axis=1)
    turn = 2.0 * np.pi * np.arange(8)[:, None] * p / 4096.0
    small = lambda x: x.astype(np.float32).astype(BF16)
    return small(folded), small(ends), np.cos(turn).astype(np.float32), np.sin(turn).astype(np.float32)


def real_dft16(a, b):
    c = math.sqrt(0.5)
    c1, c3 = math.cos(math.pi / 8), math.cos(3 * math.pi / 8)
    s1, s3 = math.sin(math.pi / 8), math.sin(3 * math.pi / 8)
    p08, m08 = a[0] + a[8], a[0] - a[8]
    s26, d26 = a[2] + a[6], (a[2] - a[6]) * c
    s17, d17, s35, d35 = a[1] + a[7], a[1] - a[7], a[3] + a[5], a[3] - a[5]
    even = [p08 + a[4] + s26, m08 + d26, p08 - a[4], m08 - d26, p08 + a[4] - s26]
    odd = [s17 + s35, d17 * c1 + d35 * c3, (s17 - s35) * c, d17 * c3 - d35 * c1]
    cosine = [None] * 9
    for p in range(4):
        cosine[p] = even[p] + odd[p]
        cosine[8 - p] = even[p] - odd[p]
    cosine[4] = even[4]
    t17, u17, t35, u35 = b[1] + b[7], b[1] - b[7], b[3] + b[5], b[3] - b[5]
    t26, u26 = (b[2] + b[6]) * c, b[2] - b[6]
    bo = [None, t17 * s1 + t35 * s3, (u17 + u35) * c, t17 * s3 - t35 * s1]
    be = [None, t26 + b[4], u26, t26 - b[4]]
    sine = [None] * 8
    for p in range(1, 4):
        sine[p] = bo[p] + be[p]
        sine[8 - p] = bo[p] - be[p]
    sine[4] = u17 - u35
    out = [None] * 16
    out[0], out[8] = cosine[0], cosine[8]
    for p in range(1, 8):
        out[p] = cosine[p] - sine[p]
        out[16 - p] = cosine[p] + sine[p]
    return out


def lagrange_weights(position):
    shifted = position + 1.0
    minus_one = position - 1.0
    minus_two = position - 2.0
    return (
        -position * minus_one * minus_two / 6.0,
        shifted * minus_one * minus_two / 2.0,
        -shifted * position * minus_two / 2.0,
        shifted * position * minus_one / 6.0,
    )


def circle_kernel(
    got, folded, single, tcos, tsin, out,
    wide, left, left0, left8, field, field0, field8, tiles, grid_o, grid_w, ends, mark, ids_v, ids_s, sem,
):
    wide[...] = got[...].astype(F32)
    for s in range(2):
        flipped = jnp.transpose(wide[pl.ds(8 + 9 * s, 128, stride=18), :])
        ids_v[8 * s : 8 * s + 8, :] = flipped[96:104, :].astype(I32) & 63
    copy = pltpu.make_async_copy(ids_v, ids_s, sem)
    copy.start()
    for i in range(2):
        for g in range(8):
            flipped = jnp.transpose(wide[pl.ds(9 * i + g, 128, stride=18), :].astype(BF16))
            for odd in range(2):
                e = 2 * g + odd
                if e % 8 == 0:
                    to, row, lane0 = (left0 if e == 0 else left8), 32 * i, 0
                else:
                    to, row, lane0 = left, (min(e, 16 - e) - 1) * 64 + 32 * i, 0 if e < 8 else 256
                to[row : row + 32, lane0 : lane0 + 128] = flipped[64 * odd : 64 * odd + 32]
                to[row : row + 32, lane0 + 128 : lane0 + 256] = flipped[64 * odd + 32 : 64 * odd + 64]
    field[...] = jnp.dot(left[...], folded[...], preferred_element_type=F32)
    field0[...] = jnp.dot(left0[...], single[:, 0:256], preferred_element_type=F32)
    field8[...] = jnp.dot(left8[...], single[:, 256:512], preferred_element_type=F32)
    for half in range(2):
        re = slice(128 * half, 128 * half + 128)
        im = slice(256 + 128 * half, 256 + 128 * half + 128)
        for r in range(4):
            a, b = [field0[16 * r : 16 * r + 16, re]], [None]
            for e in range(1, 8):
                row = slice(64 * (e - 1) + 16 * r, 64 * (e - 1) + 16 * r + 16)
                yr, yi = field[row, re], field[row, im]
                tc, ts = tcos[e : e + 1, re], tsin[e : e + 1, re]
                a.append(yr * tc - yi * ts)
                b.append(yr * ts + yi * tc)
            a.append(field8[16 * r : 16 * r + 16, re])
            i, j = r // 2, r % 2
            for p, x in enumerate(real_dft16(a, b)):
                tiles[32 * i + 2 * p + half, 16 * j : 16 * j + 16, :] = x.astype(BF16)
    part = lanes_of((64, 128)) // 32
    o = jnp.zeros((64, 128), F32)
    f = jnp.zeros((64, 128), F32)
    for n in range(2):
        for s in range(2):
            x = wide[pl.ds(18 * n + 8 + 9 * s, 64, stride=36), :]
            to = 2 * n + s
            o = jnp.where(part == to, pltpu.roll(x, 32 * to, 1), o)
            y = x + pltpu.roll(x, 96, 1)
            f = jnp.where(part == to, pltpu.roll(y, (32 * to + 96) % 128, 1), f)
    grid_o[...] = o
    for place, w in enumerate(lagrange_weights(f)):
        grid_w[place] = w
    part = lanes_of((128, 128)) // 32
    one = wide[pl.ds(8, 128, stride=18), :]
    two = wide[pl.ds(17, 128, stride=18), :]
    mark[...] = jnp.where(
        part < 2,
        jnp.where(part == 0, pltpu.roll(one, 32, 1), pltpu.roll(two, 64, 1)),
        jnp.where(part == 2, pltpu.roll(one, 96, 1), two),
    )
    ends[0] = jnp.zeros((8, 128), F32)
    ends[129] = jnp.zeros((8, 128), F32)
    copy.wait()
    sub = lax.broadcasted_iota(I32, (128, 128), 0).astype(F32).astype(BF16)
    lane32 = lanes_of((32, 128)) // 32
    low16 = lanes_of((16, 128)) < 64
    even8 = (lanes_of((8, 128)) // 32) % 2 == 0

    def pair(t, carry):
        row = lambda ref: jnp.broadcast_to(ref[pl.ds(t, 1), :], (128, 128)).astype(BF16)
        distance = sub - row(grid_o)
        matrix = jnp.zeros((128, 128), BF16)
        for place in range(4):
            matrix = jnp.where(distance == place, row(grid_w.at[place]), matrix)
        stack = jnp.concatenate(
            [tiles[ids_s[8 * s, 2 * t + n]] for n in range(2) for s in range(2)], axis=0
        )
        res = jnp.dot(stack, matrix, preferred_element_type=F32)
        d = res[0:32]
        for q in range(1, 4):
            d = jnp.where(lane32 == q, res[32 * q : 32 * q + 32], d)
        a, b = d[0:16], d[16:32]
        for n in range(2):
            m = 2 * t + n
            x = jnp.where(low16, a, pltpu.roll(b, 64, 1)) if n == 0 else jnp.where(low16, pltpu.roll(a, 64, 1), b)
            out[m, 0:16, :] = x.astype(BF16)
            x = jnp.where(mark[pl.ds(m, 1), :] >= 64.0, x, 0.0)
            x = x + pltpu.roll(x, 96, 1)
            ends[m + 1] = jnp.where(even8, x[0:8], pltpu.roll(x[8:16], 32, 1))
        return carry

    lax.fori_loop(0, 64, pair, 0, unroll=16)
    tail = lanes_of((8, 128)) % 32 >= 16

    def rims(n, carry):
        out[n, 16:24, :] = jnp.where(tail, ends[n], ends[n + 2]).astype(BF16)
        return carry

    lax.fori_loop(0, 128, rims, 0, unroll=16)


def circle_call(got):
    folded, single, tcos, tsin = tables()
    vmem = pl.BlockSpec(memory_space=pltpu.VMEM)
    return pl.pallas_call(
        circle_kernel,
        in_specs=[vmem] * 5,
        out_specs=vmem,
        out_shape=pltpu.VMEM((128, 24, 128), BF16),
        scratch_shapes=[
            pltpu.VMEM((2304, 128), F32),
            pltpu.VMEM((448, 512), BF16),
            pltpu.VMEM((64, 256), BF16),
            pltpu.VMEM((64, 256), BF16),
            pltpu.VMEM((448, 512), F32),
            pltpu.VMEM((64, 256), F32),
            pltpu.VMEM((64, 256), F32),
            pltpu.VMEM((64, 32, 128), BF16),
            pltpu.VMEM((64, 128), F32),
            pltpu.VMEM((4, 64, 128), F32),
            pltpu.VMEM((130, 8, 128), F32),
            pltpu.VMEM((128, 128), F32),
            pltpu.VMEM((16, 128), I32),
            pltpu.SMEM((16, 128), I32),
            pltpu.SemaphoreType.DMA,
        ],
        name="circle",
    )(near(got), *[near(jnp.asarray(x)) for x in (folded, single, tcos, tsin)])


def circulant(v):
    x = jnp.broadcast_to(v, (128, 128))
    sub = lax.broadcasted_iota(I32, (128, 128), 0)
    for bit in range(7):
        x = jnp.where((lax.shift_right_logical(sub, bit) & 1) == 1, pltpu.roll(x, 1 << bit, 1), x)
    return x


def two_parts(x):
    hi = x.astype(BF16)
    return hi, (x - hi.astype(F32)).astype(BF16)


def signal_kernel(flat, came, v, out, line, result):
    lane = lanes_of((16, 128)) // 32
    lane32 = lanes_of((32, 128))

    def add(h, total):
        return total + came[h, 16:24, :].astype(F32)

    total = lax.fori_loop(0, 128, add, jnp.zeros((8, 128), F32), unroll=16)
    rim = jnp.concatenate([total] + [pltpu.roll(total, 128 - 32 * j, 1) for j in range(1, 4)], axis=0)
    before = pltpu.roll(rim, 96, 1).astype(BF16)
    after = rim.astype(BF16)

    def block(b, carry):
        older, newer = carry
        low = jnp.zeros((16, 128), F32)
        high = jnp.zeros((16, 128), F32)
        for q in range(4):
            at = flat[4 * b + q]
            x = came[lax.shift_right_logical(at, 1), 0:16, :].astype(F32)
            shift = (32 * q - 32 * (at & 1)) & 127
            low = jnp.where(lane == q, pltpu.roll(x, shift, 1), low)
            high = jnp.where(lane == q, pltpu.roll(x, shift ^ 64, 1), high)
        x = jnp.concatenate([low, high], axis=0).astype(BF16)
        line[b + 1, :, 0:128] = x
        line[b, :, 128:256] = jnp.where(lane32 < 64, x, older)
        return newer, x

    older, newer = lax.fori_loop(0, 32, block, (jnp.zeros((32, 128), BF16), before), unroll=4)
    line[32, :, 128:256] = jnp.where(lane32 < 64, after, older)
    ring = circulant(v[...])
    gap = lanes_of((128, 128)) - lax.broadcasted_iota(I32, (128, 128), 0)
    near = (gap >= -64) & (gap <= 64)
    hi, lo = two_parts(jnp.concatenate([jnp.where(near, ring, 0.0), jnp.where(near, 0.0, ring)], axis=0))
    result[...] = jnp.dot(
        line[1:33].reshape(1024, 256), jnp.concatenate([hi, lo], axis=1), preferred_element_type=F32
    )
    for b in range(32):
        y = result[32 * b : 32 * b + 32, :]
        out[:, 128 * b : 128 * b + 128] = y[:, 0:128] + y[:, 128:256]


def signal_call(flat, came, v):
    vmem = pl.BlockSpec(memory_space=pltpu.VMEM)
    return pl.pallas_call(
        signal_kernel,
        in_specs=[pl.BlockSpec(memory_space=pltpu.SMEM), vmem, vmem],
        out_specs=vmem,
        out_shape=jax.ShapeDtypeStruct((32, 4096), F32),
        scratch_shapes=[pltpu.VMEM((33, 32, 256), BF16), pltpu.VMEM((1024, 256), F32)],
        name="signal",
    )(flat, near(came), near(v))


def local(wigner, alm, beam, crossing, offsets, fraction, taps):
    det = lax.axis_index("det").astype(I32).reshape(1)
    order = lax.axis_index("ord").astype(I32).reshape(1)
    beams = beam.reshape(64, 2, 16, 128).transpose(0, 2, 1, 3).reshape(64, 32, 128)
    keep, send, flat = spectra_call(
        det, order, wigner, alm, beams, crossing, offsets.reshape(32, 128), fraction.reshape(32, 128)
    )
    partner = lax.ppermute(send, "det", [(0, 1), (1, 0)])
    message = (keep + partner).astype(BF16).reshape(ORD, ROWS, 2, 128)
    arrived = lax.all_to_all(message, "ord", split_axis=0, concat_axis=0, tiled=True)
    outgoing = circle_call(arrived.reshape(ORD * 2 * ROWS, 128))
    came = lax.all_to_all(outgoing, "ord", split_axis=0, concat_axis=0, tiled=True)
    v = jnp.concatenate([taps[16::-1], jnp.zeros((95,), F32), taps[:16:-1]]).reshape(1, 128)
    return signal_call(flat.reshape(128), came, v)


def solution(mesh):
    return jax.shard_map(
        local,
        mesh=mesh,
        in_specs=(
            P("ord", None, None, "det"),
            P("ord", None, None),
            P(),
            P("ord", None),
            P("ord", None),
            P("ord", None),
            P(),
        ),
        out_specs=P("det", "ord"),
        check_vma=False,
    )
```

```python
import math

import jax
import jax.numpy as jnp
import numpy as np
from jax import lax
from jax.experimental import pallas as pl
from jax.experimental.pallas import tpu as pltpu
from jax.sharding import PartitionSpec as P

F32 = jnp.float32
BF16 = jnp.bfloat16
I32 = jnp.int32

ORD = 128
ROWS = 9
NT = (((1,), (1,)), ((), ()))


def lanes_of(shape):
    return lax.broadcasted_iota(I32, shape, len(shape) - 1)


def near(x):
    return pltpu.with_memory_space_constraint(x, pltpu.VMEM)


def circulant(v):
    x = jnp.broadcast_to(v, (128, 128))
    sub = lax.broadcasted_iota(I32, (128, 128), 0)
    for bit in range(7):
        x = jnp.where((lax.shift_right_logical(sub, bit) & 1) == 1, pltpu.roll(x, 1 << bit, 1), x)
    return x


def two_parts(x):
    hi = x.astype(BF16)
    return hi, (x - hi.astype(F32)).astype(BF16)


def spectra_kernel(
    det_ref, ord_ref, wig_hbm, alm_hbm, beam_hbm, cross_hbm, offset_hbm, fraction_hbm, taps_hbm, keep, send, flat, weights,
    wig, alm, beam, crossing, offsets, fraction, taps, cells, wide, beams, product, found, sems,
):
    det = det_ref[0]
    half_lanes = pl.ds(pl.multiple_of(1024 * det, 1024), 1024)
    copies = [
        pltpu.make_async_copy(beam_hbm.at[:, pl.ds(pl.multiple_of(16 * det, 16), 16), :], beam, sems.at[8]),
        pltpu.make_async_copy(cross_hbm, crossing, sems.at[9]),
        pltpu.make_async_copy(offset_hbm, offsets, sems.at[10]),
        pltpu.make_async_copy(fraction_hbm, fraction, sems.at[11]),
        pltpu.make_async_copy(alm_hbm.at[:, :, half_lanes], alm, sems.at[12]),
    ]
    coefficients = pltpu.make_async_copy(taps_hbm, taps, sems.at[13])
    coefficients.start()
    block = lambda g: pltpu.make_async_copy(wig_hbm.at[pl.ds(2 * g, 2)], wig.at[pl.ds(2 * g, 2)], sems.at[g])
    for copy in copies:
        copy.start()
    for g in range(8):
        block(g).start()

    def build(slot, k, m):
        for half in range(2):
            for c in range(2):
                row = alm[m, c : c + 1, :]
                at = 64 * half + 32 * c
                product[slot, at : at + 32, :] = beams[k, 32 * half : 32 * half + 32, :] * row

    def prepare():
        copies[0].wait()
        wide[...] = beam[...].astype(F32).reshape(1024, 128)
        for half in range(2):
            base = (32 * det if half == 0 else 32 * (1 - det)) * 16
            for k in range(2):
                for t in range(8):
                    x = wide[pl.ds(base + 2 * t + k, 32, stride=16), :]
                    beams[k, 32 * half : 32 * half + 32, 128 * t : 128 * t + 128] = x.astype(BF16)
        for copy in copies[1:4]:
            copy.wait()
        c = crossing[...]
        holder = lax.shift_right_logical(c, 6)
        across = jnp.broadcast_to(holder, (128, 128)).astype(F32)
        down = jnp.transpose(across)
        sub = lax.broadcasted_iota(I32, (128, 128), 0)
        lane = lanes_of((128, 128))
        earlier = jnp.where((across == down) & (sub < lane), 1.0, 0.0)
        slot = jnp.sum(earlier, axis=0, keepdims=True).astype(I32)
        flat[...] = holder * 2 + slot
        o32 = offsets[...].astype(F32)
        f32_ = fraction[...]
        hi = f32_.astype(BF16).astype(F32)
        lo = f32_ - hi
        lane32 = lanes_of((32, 128))
        ids = jnp.broadcast_to((c & 63).astype(F32), (128, 128))
        ids = jnp.sum(jnp.where(sub == lane, ids, 0.0), axis=1, keepdims=True)
        end = ((lane < 112) & (sub == 0)) | ((lane >= 112) & (sub == 127))
        ids = jnp.broadcast_to(ids, (128, 128)) + jnp.where(end, 64.0, 0.0)
        for part in range(4):
            sh = 128 - 32 * part
            row = jnp.where(
                lane32 < 32,
                pltpu.roll(o32, sh % 128, 1),
                jnp.where(
                    lane32 < 64, pltpu.roll(hi, (sh + 32) % 128, 1), pltpu.roll(lo, (sh + 64) % 128, 1)
                ),
            )
            cells[pl.ds(part, 32, stride=4), :] = row
        data = jnp.where(lane < 96, cells[...], ids).astype(BF16)
        for s in range(2):
            pick = jnp.where((sub == holder) & (slot == s), 1.0, 0.0).astype(BF16)
            got = jnp.dot(pick, data, preferred_element_type=F32)
            keep[pl.ds(8 + 9 * s, 128, stride=18), :] = got
            send[pl.ds(8 + 9 * s, 128, stride=18), :] = jnp.zeros((128, 128), F32)

    lane = lanes_of((128, 128))

    def place(step, from_):
        first = jnp.where((ord_ref[0] == 0) & (step == 0), 1.0 / 64.0, 1.0 / 32.0)
        for k in range(2):
            one = found[from_ + 2 * k] * first
            two = found[from_ + 2 * k + 1] * (1.0 / 32.0)
            row = pl.ds(k * 1152 + step, 128, stride=9)
            keep[row, :] = jnp.where(lane < 64, one, pltpu.roll(two, 64, 1))
            send[row, :] = jnp.where(lane < 64, pltpu.roll(one, 64, 1), two)

    coefficients.wait()
    at = lanes_of((1, 128))
    v = jnp.zeros((1, 128), F32)
    for lag in range(33):
        v = jnp.where(at == (16 - lag) % 128, taps[lag], v)
    ring = circulant(v)
    gap = lanes_of((128, 128)) - lax.broadcasted_iota(I32, (128, 128), 0)
    near = (gap >= -64) & (gap <= 64)
    hi, lo = two_parts(jnp.concatenate([jnp.where(near, ring, 0.0), jnp.where(near, 0.0, ring)], axis=0))
    weights[...] = jnp.concatenate([hi, lo], axis=1)
    prepare()
    copies[4].wait()

    def step(t, carry):
        block(2 * t).wait()
        block(2 * t + 1).wait()
        for part in range(2):
            place(jnp.maximum(2 * t - 2, 0) + part, 4 * part)
        for unit in range(8):
            g, k, e = 2 * t + unit // 4, unit // 2 % 2, unit % 2
            build(unit % 4, k, 2 * g + e)
            found[unit] = lax.dot_general(wig[2 * g + e, k], product[unit % 4], NT, preferred_element_type=F32)
        return carry

    lax.fori_loop(0, 4, step, 0)
    place(6, 0)
    place(7, 4)


def spectra_call(det, order, wig, alm, beam, crossing, offsets, fraction, taps):
    smem = pl.BlockSpec(memory_space=pltpu.SMEM)
    vmem = pl.BlockSpec(memory_space=pltpu.VMEM)
    return pl.pallas_call(
        spectra_kernel,
        in_specs=[smem, smem] + [pl.BlockSpec(memory_space=pl.ANY)] * 7,
        out_specs=[vmem] * 4,
        out_shape=[
            pltpu.VMEM((2304, 128), F32),
            pltpu.VMEM((2304, 128), F32),
            jax.ShapeDtypeStruct((1, 128), I32),
            pltpu.VMEM((256, 256), BF16),
        ],
        scratch_shapes=[
            pltpu.VMEM((16, 2, 128, 1024), BF16),
            pltpu.VMEM((16, 2, 1024), BF16),
            pltpu.VMEM((64, 16, 128), BF16),
            pltpu.VMEM((1, 128), I32),
            pltpu.VMEM((32, 128), I32),
            pltpu.VMEM((32, 128), F32),
            pltpu.SMEM((33,), F32),
            pltpu.VMEM((128, 128), F32),
            pltpu.VMEM((1024, 128), F32),
            pltpu.VMEM((2, 64, 1024), BF16),
            pltpu.VMEM((4, 128, 1024), BF16),
            pltpu.VMEM((8, 128, 128), F32),
            pltpu.SemaphoreType.DMA((14,)),
        ],
        name="spectra",
    )(det, order, wig, alm, beam, crossing, offsets, fraction, taps)


def tables():
    d = np.arange(128)[:, None]
    p = np.arange(256)[None, :]
    here = 2.0 * np.pi * ((d * p) % 256) / 256.0
    after = 2.0 * np.pi * (((d + 1) * p) % 256) / 256.0
    eighth = here + 2.0 * np.pi * 8 * p / 4096.0
    cat = np.concatenate
    real = cat([np.cos(here), -np.sin(here), np.cos(after), -np.sin(after)], axis=0)
    imag = cat([np.sin(here), np.cos(here), -np.sin(after), -np.cos(after)], axis=0)
    folded = cat([real, imag], axis=1)
    ends = cat([cat([np.cos(x), -np.sin(x)], axis=0) for x in (here, eighth)], axis=1)
    turn = 2.0 * np.pi * np.arange(8)[:, None] * p / 4096.0
    small = lambda x: x.astype(np.float32).astype(BF16)
    return small(folded), small(ends), np.cos(turn).astype(np.float32), np.sin(turn).astype(np.float32)


def real_dft16(a, b):
    c = math.sqrt(0.5)
    c1, c3 = math.cos(math.pi / 8), math.cos(3 * math.pi / 8)
    s1, s3 = math.sin(math.pi / 8), math.sin(3 * math.pi / 8)
    p08, m08 = a[0] + a[8], a[0] - a[8]
    s26, d26 = a[2] + a[6], (a[2] - a[6]) * c
    s17, d17, s35, d35 = a[1] + a[7], a[1] - a[7], a[3] + a[5], a[3] - a[5]
    even = [p08 + a[4] + s26, m08 + d26, p08 - a[4], m08 - d26, p08 + a[4] - s26]
    odd = [s17 + s35, d17 * c1 + d35 * c3, (s17 - s35) * c, d17 * c3 - d35 * c1]
    cosine = [None] * 9
    for p in range(4):
        cosine[p] = even[p] + odd[p]
        cosine[8 - p] = even[p] - odd[p]
    cosine[4] = even[4]
    t17, u17, t35, u35 = b[1] + b[7], b[1] - b[7], b[3] + b[5], b[3] - b[5]
    t26, u26 = (b[2] + b[6]) * c, b[2] - b[6]
    bo = [None, t17 * s1 + t35 * s3, (u17 + u35) * c, t17 * s3 - t35 * s1]
    be = [None, t26 + b[4], u26, t26 - b[4]]
    sine = [None] * 8
    for p in range(1, 4):
        sine[p] = bo[p] + be[p]
        sine[8 - p] = bo[p] - be[p]
    sine[4] = u17 - u35
    out = [None] * 16
    out[0], out[8] = cosine[0], cosine[8]
    for p in range(1, 8):
        out[p] = cosine[p] - sine[p]
        out[16 - p] = cosine[p] + sine[p]
    return out


def lagrange_weights(position):
    shifted = position + 1.0
    minus_one = position - 1.0
    minus_two = position - 2.0
    return (
        -position * minus_one * minus_two / 6.0,
        shifted * minus_one * minus_two / 2.0,
        -shifted * position * minus_two / 2.0,
        shifted * position * minus_one / 6.0,
    )


def circle_kernel(
    got, folded, single, tcos, tsin, out,
    wide, left, left0, left8, field, field0, field8, tiles, grid_o, grid_w, ends, mark, ids_v, ids_s, sem,
):
    wide[...] = got[...].astype(F32)
    for s in range(2):
        flipped = jnp.transpose(wide[pl.ds(8 + 9 * s, 128, stride=18), :])
        ids_v[8 * s : 8 * s + 8, :] = flipped[96:104, :].astype(I32) & 63
    copy = pltpu.make_async_copy(ids_v, ids_s, sem)
    copy.start()
    for i in range(2):
        for g in range(8):
            flipped = jnp.transpose(wide[pl.ds(9 * i + g, 128, stride=18), :].astype(BF16))
            for odd in range(2):
                e = 2 * g + odd
                if e % 8 == 0:
                    to, row, lane0 = (left0 if e == 0 else left8), 32 * i, 0
                else:
                    to, row, lane0 = left, (min(e, 16 - e) - 1) * 64 + 32 * i, 0 if e < 8 else 256
                to[row : row + 32, lane0 : lane0 + 128] = flipped[64 * odd : 64 * odd + 32]
                to[row : row + 32, lane0 + 128 : lane0 + 256] = flipped[64 * odd + 32 : 64 * odd + 64]
    field[...] = jnp.dot(left[...], folded[...], preferred_element_type=F32)
    field0[...] = jnp.dot(left0[...], single[:, 0:256], preferred_element_type=F32)
    field8[...] = jnp.dot(left8[...], single[:, 256:512], preferred_element_type=F32)
    for half in range(2):
        re = slice(128 * half, 128 * half + 128)
        im = slice(256 + 128 * half, 256 + 128 * half + 128)
        for r in range(4):
            a, b = [field0[16 * r : 16 * r + 16, re]], [None]
            for e in range(1, 8):
                row = slice(64 * (e - 1) + 16 * r, 64 * (e - 1) + 16 * r + 16)
                yr, yi = field[row, re], field[row, im]
                tc, ts = tcos[e : e + 1, re], tsin[e : e + 1, re]
                a.append(yr * tc - yi * ts)
                b.append(yr * ts + yi * tc)
            a.append(field8[16 * r : 16 * r + 16, re])
            i, j = r // 2, r % 2
            for p, x in enumerate(real_dft16(a, b)):
                tiles[32 * i + 2 * p + half, 16 * j : 16 * j + 16, :] = x.astype(BF16)
    part = lanes_of((64, 128)) // 32
    o = jnp.zeros((64, 128), F32)
    f = jnp.zeros((64, 128), F32)
    for n in range(2):
        for s in range(2):
            x = wide[pl.ds(18 * n + 8 + 9 * s, 64, stride=36), :]
            to = 2 * n + s
            o = jnp.where(part == to, pltpu.roll(x, 32 * to, 1), o)
            y = x + pltpu.roll(x, 96, 1)
            f = jnp.where(part == to, pltpu.roll(y, (32 * to + 96) % 128, 1), f)
    grid_o[...] = o
    for place, w in enumerate(lagrange_weights(f)):
        grid_w[place] = w
    part = lanes_of((128, 128)) // 32
    one = wide[pl.ds(8, 128, stride=18), :]
    two = wide[pl.ds(17, 128, stride=18), :]
    mark[...] = jnp.where(
        part < 2,
        jnp.where(part == 0, pltpu.roll(one, 32, 1), pltpu.roll(two, 64, 1)),
        jnp.where(part == 2, pltpu.roll(one, 96, 1), two),
    )
    ends[0] = jnp.zeros((8, 128), F32)
    ends[129] = jnp.zeros((8, 128), F32)
    copy.wait()
    sub = lax.broadcasted_iota(I32, (128, 128), 0).astype(F32).astype(BF16)
    lane32 = lanes_of((32, 128)) // 32
    low16 = lanes_of((16, 128)) < 64
    even8 = (lanes_of((8, 128)) // 32) % 2 == 0

    def pair(t, carry):
        row = lambda ref: jnp.broadcast_to(ref[pl.ds(t, 1), :], (128, 128)).astype(BF16)
        distance = sub - row(grid_o)
        matrix = jnp.zeros((128, 128), BF16)
        for place in range(4):
            matrix = jnp.where(distance == place, row(grid_w.at[place]), matrix)
        stack = jnp.concatenate(
            [tiles[ids_s[8 * s, 2 * t + n]] for n in range(2) for s in range(2)], axis=0
        )
        res = jnp.dot(stack, matrix, preferred_element_type=F32)
        d = res[0:32]
        for q in range(1, 4):
            d = jnp.where(lane32 == q, res[32 * q : 32 * q + 32], d)
        a, b = d[0:16], d[16:32]
        for n in range(2):
            m = 2 * t + n
            x = jnp.where(low16, a, pltpu.roll(b, 64, 1)) if n == 0 else jnp.where(low16, pltpu.roll(a, 64, 1), b)
            out[m, 0:16, :] = x.astype(BF16)
            x = jnp.where(mark[pl.ds(m, 1), :] >= 64.0, x, 0.0)
            x = x + pltpu.roll(x, 96, 1)
            ends[m + 1] = jnp.where(even8, x[0:8], pltpu.roll(x[8:16], 32, 1))
        return carry

    lax.fori_loop(0, 64, pair, 0, unroll=32)
    tail = lanes_of((8, 128)) % 32 >= 16

    def rims(n, carry):
        out[n, 16:24, :] = jnp.where(tail, ends[n], ends[n + 2]).astype(BF16)
        return carry

    lax.fori_loop(0, 128, rims, 0, unroll=16)


def circle_call(got):
    folded, single, tcos, tsin = tables()
    vmem = pl.BlockSpec(memory_space=pltpu.VMEM)
    return pl.pallas_call(
        circle_kernel,
        in_specs=[vmem] * 5,
        out_specs=vmem,
        out_shape=pltpu.VMEM((128, 24, 128), BF16),
        scratch_shapes=[
            pltpu.VMEM((2304, 128), F32),
            pltpu.VMEM((448, 512), BF16),
            pltpu.VMEM((64, 256), BF16),
            pltpu.VMEM((64, 256), BF16),
            pltpu.VMEM((448, 512), F32),
            pltpu.VMEM((64, 256), F32),
            pltpu.VMEM((64, 256), F32),
            pltpu.VMEM((64, 32, 128), BF16),
            pltpu.VMEM((64, 128), F32),
            pltpu.VMEM((4, 64, 128), F32),
            pltpu.VMEM((130, 8, 128), F32),
            pltpu.VMEM((128, 128), F32),
            pltpu.VMEM((16, 128), I32),
            pltpu.SMEM((16, 128), I32),
            pltpu.SemaphoreType.DMA,
        ],
        name="circle",
    )(near(got), *[near(jnp.asarray(x)) for x in (folded, single, tcos, tsin)])


def signal_kernel(flat_any, came, weights, out_any, flat, line, result, out, sems):
    slots = pltpu.make_async_copy(flat_any, flat, sems.at[4])
    slots.start()
    lane = lanes_of((16, 128)) // 32
    lane32 = lanes_of((32, 128))

    def add(h, total):
        return total + came[h, 16:24, :].astype(F32)

    total = lax.fori_loop(0, 128, add, jnp.zeros((8, 128), F32), unroll=16)
    rim = jnp.concatenate([total] + [pltpu.roll(total, 128 - 32 * j, 1) for j in range(1, 4)], axis=0)
    before = pltpu.roll(rim, 96, 1).astype(BF16)
    after = rim.astype(BF16)

    slots.wait()

    def block(b, carry):
        older, newer = carry
        low = jnp.zeros((16, 128), F32)
        high = jnp.zeros((16, 128), F32)
        for q in range(4):
            at = flat[0, 4 * b + q]
            x = came[lax.shift_right_logical(at, 1), 0:16, :].astype(F32)
            shift = (32 * q - 32 * (at & 1)) & 127
            low = jnp.where(lane == q, pltpu.roll(x, shift, 1), low)
            high = jnp.where(lane == q, pltpu.roll(x, shift ^ 64, 1), high)
        x = jnp.concatenate([low, high], axis=0).astype(BF16)
        line[b + 1, :, 0:128] = x
        line[b, :, 128:256] = jnp.where(lane32 < 64, x, older)
        return newer, x

    older, newer = lax.fori_loop(0, 32, block, (jnp.zeros((32, 128), BF16), before), unroll=4)
    line[32, :, 128:256] = jnp.where(lane32 < 64, after, older)
    copies = []
    for part in range(4):
        result[...] = jnp.dot(
            line[1 + 8 * part : 9 + 8 * part].reshape(256, 256), weights[...], preferred_element_type=F32
        )
        for b in range(8):
            y = result[32 * b : 32 * b + 32, :]
            out[part, :, 128 * b : 128 * b + 128] = y[:, 0:128] + y[:, 128:256]
        copies.append(
            pltpu.make_async_copy(out.at[part], out_any.at[:, pl.ds(1024 * part, 1024)], sems.at[part])
        )
        copies[-1].start()
    for copy in copies:
        copy.wait()


def signal_call(flat, came, weights):
    vmem = pl.BlockSpec(memory_space=pltpu.VMEM)
    return pl.pallas_call(
        signal_kernel,
        in_specs=[pl.BlockSpec(memory_space=pl.ANY), vmem, vmem],
        out_specs=pl.BlockSpec(memory_space=pl.ANY),
        out_shape=jax.ShapeDtypeStruct((32, 4096), F32),
        scratch_shapes=[
            pltpu.SMEM((1, 128), I32),
            pltpu.VMEM((33, 32, 256), BF16),
            pltpu.VMEM((256, 256), F32),
            pltpu.VMEM((4, 32, 1024), F32),
            pltpu.SemaphoreType.DMA((5,)),
        ],
        name="signal",
    )(flat, near(came), near(weights))


def local(wigner, alm, beam, crossing, offsets, fraction, taps):
    det = lax.axis_index("det").astype(I32).reshape(1)
    order = lax.axis_index("ord").astype(I32).reshape(1)
    beams = beam.reshape(64, 2, 16, 128).transpose(0, 2, 1, 3).reshape(64, 32, 128)
    keep, send, flat, weights = spectra_call(
        det, order, wigner, alm, beams, crossing, offsets.reshape(32, 128), fraction.reshape(32, 128), taps
    )
    partner = lax.ppermute(send, "det", [(0, 1), (1, 0)])
    message = (keep + partner).astype(BF16).reshape(ORD, ROWS, 2, 128)
    arrived = lax.all_to_all(message, "ord", split_axis=0, concat_axis=0, tiled=True)
    outgoing = circle_call(arrived.reshape(ORD * 2 * ROWS, 128))
    came = lax.all_to_all(outgoing, "ord", split_axis=0, concat_axis=0, tiled=True)
    return signal_call(flat, came, weights)


def solution(mesh):
    return jax.shard_map(
        local,
        mesh=mesh,
        in_specs=(
            P("ord", None, None, "det"),
            P("ord", None, None),
            P(),
            P("ord", None),
            P("ord", None),
            P("ord", None),
            P(),
        ),
        out_specs=P("det", "ord"),
        check_vma=False,
    )
```

```python
import math

import jax
import jax.numpy as jnp
import numpy as np
from jax import lax
from jax.experimental import pallas as pl
from jax.experimental.pallas import tpu as pltpu
from jax.sharding import PartitionSpec as P

F32 = jnp.float32
BF16 = jnp.bfloat16
I32 = jnp.int32

ORD = 128
ROWS = 9
NT = (((1,), (1,)), ((), ()))


def lanes_of(shape):
    return lax.broadcasted_iota(I32, shape, len(shape) - 1)


def near(x):
    return pltpu.with_memory_space_constraint(x, pltpu.VMEM)


def circulant(v):
    x = jnp.broadcast_to(v, (128, 128))
    sub = lax.broadcasted_iota(I32, (128, 128), 0)
    for bit in range(7):
        x = jnp.where((lax.shift_right_logical(sub, bit) & 1) == 1, pltpu.roll(x, 1 << bit, 1), x)
    return x


def two_parts(x):
    hi = x.astype(BF16)
    return hi, (x - hi.astype(F32)).astype(BF16)


def spectra_kernel(
    det_ref, ord_ref, wig_hbm, alm_hbm, beam_hbm, cross_hbm, offset_hbm, fraction_hbm, taps_hbm, keep, send, flat, weights,
    wig, alm, beam, crossing, offsets, fraction, taps, cells, wide, beams, product, found, sems,
):
    det = det_ref[0]
    half_lanes = pl.ds(pl.multiple_of(1024 * det, 1024), 1024)
    copies = [
        pltpu.make_async_copy(beam_hbm.at[:, pl.ds(pl.multiple_of(16 * det, 16), 16), :], beam, sems.at[8]),
        pltpu.make_async_copy(cross_hbm, crossing, sems.at[9]),
        pltpu.make_async_copy(offset_hbm, offsets, sems.at[10]),
        pltpu.make_async_copy(fraction_hbm, fraction, sems.at[11]),
        pltpu.make_async_copy(alm_hbm.at[:, :, half_lanes], alm, sems.at[12]),
    ]
    coefficients = pltpu.make_async_copy(taps_hbm, taps, sems.at[13])
    coefficients.start()
    block = lambda g: pltpu.make_async_copy(wig_hbm.at[pl.ds(2 * g, 2)], wig.at[pl.ds(2 * g, 2)], sems.at[g])
    for copy in copies:
        copy.start()
    for g in range(8):
        block(g).start()

    def build(slot, k, m):
        for half in range(2):
            for c in range(2):
                row = alm[m, c : c + 1, :]
                at = 64 * half + 32 * c
                product[slot, at : at + 32, :] = beams[k, 32 * half : 32 * half + 32, :] * row

    def prepare():
        copies[0].wait()
        wide[...] = beam[...].astype(F32).reshape(1024, 128)
        for half in range(2):
            base = (32 * det if half == 0 else 32 * (1 - det)) * 16
            for k in range(2):
                for t in range(8):
                    x = wide[pl.ds(base + 2 * t + k, 32, stride=16), :]
                    beams[k, 32 * half : 32 * half + 32, 128 * t : 128 * t + 128] = x.astype(BF16)
        for copy in copies[1:4]:
            copy.wait()
        c = crossing[...]
        holder = lax.shift_right_logical(c, 6)
        across = jnp.broadcast_to(holder, (128, 128)).astype(F32)
        down = jnp.transpose(across)
        sub = lax.broadcasted_iota(I32, (128, 128), 0)
        lane = lanes_of((128, 128))
        earlier = jnp.where((across == down) & (sub < lane), 1.0, 0.0)
        slot = jnp.sum(earlier, axis=0, keepdims=True).astype(I32)
        flat[0:1] = holder
        flat[1:2] = (32 * (lane[0:1] & 3) - 32 * slot) & 127
        o32 = offsets[...].astype(F32)
        f32_ = fraction[...]
        hi = f32_.astype(BF16).astype(F32)
        lo = f32_ - hi
        lane32 = lanes_of((32, 128))
        ids = jnp.broadcast_to((c & 63).astype(F32), (128, 128))
        ids = jnp.sum(jnp.where(sub == lane, ids, 0.0), axis=1, keepdims=True)
        end = ((lane < 112) & (sub == 0)) | ((lane >= 112) & (sub == 127))
        ids = jnp.broadcast_to(ids, (128, 128)) + jnp.where(end, 64.0, 0.0)
        for part in range(4):
            sh = 128 - 32 * part
            row = jnp.where(
                lane32 < 32,
                pltpu.roll(o32, sh % 128, 1),
                jnp.where(
                    lane32 < 64, pltpu.roll(hi, (sh + 32) % 128, 1), pltpu.roll(lo, (sh + 64) % 128, 1)
                ),
            )
            cells[pl.ds(part, 32, stride=4), :] = row
        data = jnp.where(lane < 96, cells[...], ids).astype(BF16)
        for s in range(2):
            pick = jnp.where((sub == holder) & (slot == s), 1.0, 0.0).astype(BF16)
            got = jnp.dot(pick, data, preferred_element_type=F32)
            keep[pl.ds(8 + 9 * s, 128, stride=18), :] = got
            send[pl.ds(8 + 9 * s, 128, stride=18), :] = jnp.zeros((128, 128), F32)

    lane = lanes_of((128, 128))

    def place(step, from_):
        first = jnp.where((ord_ref[0] == 0) & (step == 0), 1.0 / 64.0, 1.0 / 32.0)
        for k in range(2):
            one = found[from_ + 2 * k] * first
            two = found[from_ + 2 * k + 1] * (1.0 / 32.0)
            row = pl.ds(k * 1152 + step, 128, stride=9)
            keep[row, :] = jnp.where(lane < 64, one, pltpu.roll(two, 64, 1))
            send[row, :] = jnp.where(lane < 64, pltpu.roll(one, 64, 1), two)

    coefficients.wait()
    at = lanes_of((1, 128))
    v = jnp.zeros((1, 128), F32)
    for lag in range(33):
        v = jnp.where(at == (16 - lag) % 128, taps[lag], v)
    ring = circulant(v)
    gap = lanes_of((128, 128)) - lax.broadcasted_iota(I32, (128, 128), 0)
    near = (gap >= -64) & (gap <= 64)
    hi, lo = two_parts(jnp.concatenate([jnp.where(near, ring, 0.0), jnp.where(near, 0.0, ring)], axis=0))
    weights[...] = jnp.concatenate([hi, lo], axis=1)
    prepare()
    copies[4].wait()

    def step(t, carry):
        block(2 * t).wait()
        block(2 * t + 1).wait()
        for part in range(2):
            place(jnp.maximum(2 * t - 2, 0) + part, 4 * part)
        for unit in range(8):
            g, k, e = 2 * t + unit // 4, unit // 2 % 2, unit % 2
            build(unit % 4, k, 2 * g + e)
            found[unit] = lax.dot_general(wig[2 * g + e, k], product[unit % 4], NT, preferred_element_type=F32)
        return carry

    lax.fori_loop(0, 4, step, 0)
    place(6, 0)
    place(7, 4)


def spectra_call(det, order, wig, alm, beam, crossing, offsets, fraction, taps):
    smem = pl.BlockSpec(memory_space=pltpu.SMEM)
    vmem = pl.BlockSpec(memory_space=pltpu.VMEM)
    return pl.pallas_call(
        spectra_kernel,
        in_specs=[smem, smem] + [pl.BlockSpec(memory_space=pl.ANY)] * 7,
        out_specs=[vmem] * 4,
        out_shape=[
            pltpu.VMEM((2304, 128), F32),
            pltpu.VMEM((2304, 128), F32),
            jax.ShapeDtypeStruct((2, 128), I32),
            pltpu.VMEM((256, 256), BF16),
        ],
        scratch_shapes=[
            pltpu.VMEM((16, 2, 128, 1024), BF16),
            pltpu.VMEM((16, 2, 1024), BF16),
            pltpu.VMEM((64, 16, 128), BF16),
            pltpu.VMEM((1, 128), I32),
            pltpu.VMEM((32, 128), I32),
            pltpu.VMEM((32, 128), F32),
            pltpu.SMEM((33,), F32),
            pltpu.VMEM((128, 128), F32),
            pltpu.VMEM((1024, 128), F32),
            pltpu.VMEM((2, 64, 1024), BF16),
            pltpu.VMEM((4, 128, 1024), BF16),
            pltpu.VMEM((8, 128, 128), F32),
            pltpu.SemaphoreType.DMA((14,)),
        ],
        name="spectra",
    )(det, order, wig, alm, beam, crossing, offsets, fraction, taps)


def tables():
    d = np.arange(128)[:, None]
    p = np.arange(256)[None, :]
    here = 2.0 * np.pi * ((d * p) % 256) / 256.0
    after = 2.0 * np.pi * (((d + 1) * p) % 256) / 256.0
    eighth = here + 2.0 * np.pi * 8 * p / 4096.0
    cat = np.concatenate
    real = cat([np.cos(here), -np.sin(here), np.cos(after), -np.sin(after)], axis=0)
    imag = cat([np.sin(here), np.cos(here), -np.sin(after), -np.cos(after)], axis=0)
    folded = cat([real, imag], axis=1)
    ends = cat([cat([np.cos(x), -np.sin(x)], axis=0) for x in (here, eighth)], axis=1)
    turn = 2.0 * np.pi * np.arange(8)[:, None] * p / 4096.0
    small = lambda x: x.astype(np.float32).astype(BF16)
    return small(folded), small(ends), np.cos(turn).astype(np.float32), np.sin(turn).astype(np.float32)


def real_dft16(a, b):
    c = math.sqrt(0.5)
    c1, c3 = math.cos(math.pi / 8), math.cos(3 * math.pi / 8)
    s1, s3 = math.sin(math.pi / 8), math.sin(3 * math.pi / 8)
    p08, m08 = a[0] + a[8], a[0] - a[8]
    s26, d26 = a[2] + a[6], (a[2] - a[6]) * c
    s17, d17, s35, d35 = a[1] + a[7], a[1] - a[7], a[3] + a[5], a[3] - a[5]
    even = [p08 + a[4] + s26, m08 + d26, p08 - a[4], m08 - d26, p08 + a[4] - s26]
    odd = [s17 + s35, d17 * c1 + d35 * c3, (s17 - s35) * c, d17 * c3 - d35 * c1]
    cosine = [None] * 9
    for p in range(4):
        cosine[p] = even[p] + odd[p]
        cosine[8 - p] = even[p] - odd[p]
    cosine[4] = even[4]
    t17, u17, t35, u35 = b[1] + b[7], b[1] - b[7], b[3] + b[5], b[3] - b[5]
    t26, u26 = (b[2] + b[6]) * c, b[2] - b[6]
    bo = [None, t17 * s1 + t35 * s3, (u17 + u35) * c, t17 * s3 - t35 * s1]
    be = [None, t26 + b[4], u26, t26 - b[4]]
    sine = [None] * 8
    for p in range(1, 4):
        sine[p] = bo[p] + be[p]
        sine[8 - p] = bo[p] - be[p]
    sine[4] = u17 - u35
    out = [None] * 16
    out[0], out[8] = cosine[0], cosine[8]
    for p in range(1, 8):
        out[p] = cosine[p] - sine[p]
        out[16 - p] = cosine[p] + sine[p]
    return out


def lagrange_weights(position):
    shifted = position + 1.0
    minus_one = position - 1.0
    minus_two = position - 2.0
    return (
        -position * minus_one * minus_two / 6.0,
        shifted * minus_one * minus_two / 2.0,
        -shifted * position * minus_two / 2.0,
        shifted * position * minus_one / 6.0,
    )


def circle_kernel(
    got, folded, single, tcos, tsin, out,
    wide, left, left0, left8, field, field0, field8, tiles, grid_o, grid_w, ends, mark, ids_v, ids_s, sem,
):
    wide[...] = got[...].astype(F32)
    for s in range(2):
        flipped = jnp.transpose(wide[pl.ds(8 + 9 * s, 128, stride=18), :])
        ids_v[8 * s : 8 * s + 8, :] = flipped[96:104, :].astype(I32) & 63
    copy = pltpu.make_async_copy(ids_v, ids_s, sem)
    copy.start()
    for i in range(2):
        for g in range(8):
            flipped = jnp.transpose(wide[pl.ds(9 * i + g, 128, stride=18), :].astype(BF16))
            for odd in range(2):
                e = 2 * g + odd
                if e % 8 == 0:
                    to, row, lane0 = (left0 if e == 0 else left8), 32 * i, 0
                else:
                    to, row, lane0 = left, (min(e, 16 - e) - 1) * 64 + 32 * i, 0 if e < 8 else 256
                to[row : row + 32, lane0 : lane0 + 128] = flipped[64 * odd : 64 * odd + 32]
                to[row : row + 32, lane0 + 128 : lane0 + 256] = flipped[64 * odd + 32 : 64 * odd + 64]
    field[...] = jnp.dot(left[...], folded[...], preferred_element_type=F32)
    field0[...] = jnp.dot(left0[...], single[:, 0:256], preferred_element_type=F32)
    field8[...] = jnp.dot(left8[...], single[:, 256:512], preferred_element_type=F32)
    for half in range(2):
        re = slice(128 * half, 128 * half + 128)
        im = slice(256 + 128 * half, 256 + 128 * half + 128)
        for r in range(4):
            a, b = [field0[16 * r : 16 * r + 16, re]], [None]
            for e in range(1, 8):
                row = slice(64 * (e - 1) + 16 * r, 64 * (e - 1) + 16 * r + 16)
                yr, yi = field[row, re], field[row, im]
                tc, ts = tcos[e : e + 1, re], tsin[e : e + 1, re]
                a.append(yr * tc - yi * ts)
                b.append(yr * ts + yi * tc)
            a.append(field8[16 * r : 16 * r + 16, re])
            i, j = r // 2, r % 2
            for p, x in enumerate(real_dft16(a, b)):
                tiles[32 * i + 2 * p + half, 16 * j : 16 * j + 16, :] = x.astype(BF16)
    part = lanes_of((64, 128)) // 32
    o = jnp.zeros((64, 128), F32)
    f = jnp.zeros((64, 128), F32)
    for n in range(2):
        for s in range(2):
            x = wide[pl.ds(18 * n + 8 + 9 * s, 64, stride=36), :]
            to = 2 * n + s
            o = jnp.where(part == to, pltpu.roll(x, 32 * to, 1), o)
            y = x + pltpu.roll(x, 96, 1)
            f = jnp.where(part == to, pltpu.roll(y, (32 * to + 96) % 128, 1), f)
    grid_o[...] = o
    for place, w in enumerate(lagrange_weights(f)):
        grid_w[place] = w
    part = lanes_of((128, 128)) // 32
    one = wide[pl.ds(8, 128, stride=18), :]
    two = wide[pl.ds(17, 128, stride=18), :]
    mark[...] = jnp.where(
        part < 2,
        jnp.where(part == 0, pltpu.roll(one, 32, 1), pltpu.roll(two, 64, 1)),
        jnp.where(part == 2, pltpu.roll(one, 96, 1), two),
    )
    ends[0] = jnp.zeros((8, 128), F32)
    ends[129] = jnp.zeros((8, 128), F32)
    copy.wait()
    sub = lax.broadcasted_iota(I32, (128, 128), 0).astype(F32).astype(BF16)
    lane32 = lanes_of((32, 128)) // 32
    low16 = lanes_of((16, 128)) < 64
    even8 = (lanes_of((8, 128)) // 32) % 2 == 0

    def pair(t, carry):
        row = lambda ref: jnp.broadcast_to(ref[pl.ds(t, 1), :], (128, 128)).astype(BF16)
        distance = sub - row(grid_o)
        matrix = jnp.zeros((128, 128), BF16)
        for place in range(4):
            matrix = jnp.where(distance == place, row(grid_w.at[place]), matrix)
        stack = jnp.concatenate(
            [tiles[ids_s[8 * s, 2 * t + n]] for n in range(2) for s in range(2)], axis=0
        )
        res = jnp.dot(stack, matrix, preferred_element_type=F32)
        d = res[0:32]
        for q in range(1, 4):
            d = jnp.where(lane32 == q, res[32 * q : 32 * q + 32], d)
        a, b = d[0:16], d[16:32]
        for n in range(2):
            m = 2 * t + n
            x = jnp.where(low16, a, pltpu.roll(b, 64, 1)) if n == 0 else jnp.where(low16, pltpu.roll(a, 64, 1), b)
            out[m, 0:16, :] = x.astype(BF16)
            x = jnp.where(mark[pl.ds(m, 1), :] >= 64.0, x, 0.0)
            x = x + pltpu.roll(x, 96, 1)
            ends[m + 1] = jnp.where(even8, x[0:8], pltpu.roll(x[8:16], 32, 1))
        return carry

    lax.fori_loop(0, 64, pair, 0, unroll=32)
    tail = lanes_of((8, 128)) % 32 >= 16

    def rims(n, carry):
        out[n, 16:24, :] = jnp.where(tail, ends[n], ends[n + 2]).astype(BF16)
        return carry

    lax.fori_loop(0, 128, rims, 0, unroll=16)


def circle_call(got):
    folded, single, tcos, tsin = tables()
    vmem = pl.BlockSpec(memory_space=pltpu.VMEM)
    return pl.pallas_call(
        circle_kernel,
        in_specs=[vmem] * 5,
        out_specs=vmem,
        out_shape=pltpu.VMEM((128, 24, 128), BF16),
        scratch_shapes=[
            pltpu.VMEM((2304, 128), F32),
            pltpu.VMEM((448, 512), BF16),
            pltpu.VMEM((64, 256), BF16),
            pltpu.VMEM((64, 256), BF16),
            pltpu.VMEM((448, 512), F32),
            pltpu.VMEM((64, 256), F32),
            pltpu.VMEM((64, 256), F32),
            pltpu.VMEM((64, 32, 128), BF16),
            pltpu.VMEM((64, 128), F32),
            pltpu.VMEM((4, 64, 128), F32),
            pltpu.VMEM((130, 8, 128), F32),
            pltpu.VMEM((128, 128), F32),
            pltpu.VMEM((16, 128), I32),
            pltpu.SMEM((16, 128), I32),
            pltpu.SemaphoreType.DMA,
        ],
        name="circle",
    )(near(got), *[near(jnp.asarray(x)) for x in (folded, single, tcos, tsin)])


def signal_kernel(flat_any, came, weights, out_any, flat, line, result, out, sems):
    slots = pltpu.make_async_copy(flat_any, flat, sems.at[4])
    slots.start()
    lane = lanes_of((16, 128)) // 32
    lane32 = lanes_of((32, 128))

    def add(h, total):
        return total + came[h, 16:24, :].astype(F32)

    total = lax.fori_loop(0, 128, add, jnp.zeros((8, 128), F32), unroll=16)
    rim = jnp.concatenate([total] + [pltpu.roll(total, 128 - 32 * j, 1) for j in range(1, 4)], axis=0)
    before = pltpu.roll(rim, 96, 1).astype(BF16)
    after = rim.astype(BF16)

    slots.wait()

    def block(b, carry):
        older, newer = carry
        low = jnp.zeros((16, 128), F32)
        high = jnp.zeros((16, 128), F32)
        for q in range(4):
            x = came[flat[0, 4 * b + q], 0:16, :].astype(F32)
            shift = flat[1, 4 * b + q]
            low = jnp.where(lane == q, pltpu.roll(x, shift, 1), low)
            high = jnp.where(lane == q, pltpu.roll(x, shift ^ 64, 1), high)
        x = jnp.concatenate([low, high], axis=0).astype(BF16)
        line[b + 1, :, 0:128] = x
        line[b, :, 128:256] = jnp.where(lane32 < 64, x, older)
        return newer, x

    older, newer = lax.fori_loop(0, 32, block, (jnp.zeros((32, 128), BF16), before), unroll=16)
    line[32, :, 128:256] = jnp.where(lane32 < 64, after, older)
    copies = []
    for part in range(4):
        result[...] = jnp.dot(
            line[1 + 8 * part : 9 + 8 * part].reshape(256, 256), weights[...], preferred_element_type=F32
        )
        for b in range(8):
            y = result[32 * b : 32 * b + 32, :]
            out[part, :, 128 * b : 128 * b + 128] = y[:, 0:128] + y[:, 128:256]
        copies.append(
            pltpu.make_async_copy(out.at[part], out_any.at[:, pl.ds(1024 * part, 1024)], sems.at[part])
        )
        copies[-1].start()
    for copy in copies:
        copy.wait()


def signal_call(flat, came, weights):
    vmem = pl.BlockSpec(memory_space=pltpu.VMEM)
    return pl.pallas_call(
        signal_kernel,
        in_specs=[pl.BlockSpec(memory_space=pl.ANY), vmem, vmem],
        out_specs=pl.BlockSpec(memory_space=pl.ANY),
        out_shape=jax.ShapeDtypeStruct((32, 4096), F32),
        scratch_shapes=[
            pltpu.SMEM((2, 128), I32),
            pltpu.VMEM((33, 32, 256), BF16),
            pltpu.VMEM((256, 256), F32),
            pltpu.VMEM((4, 32, 1024), F32),
            pltpu.SemaphoreType.DMA((5,)),
        ],
        name="signal",
    )(flat, near(came), near(weights))


def local(wigner, alm, beam, crossing, offsets, fraction, taps):
    det = lax.axis_index("det").astype(I32).reshape(1)
    order = lax.axis_index("ord").astype(I32).reshape(1)
    beams = beam.reshape(64, 2, 16, 128).transpose(0, 2, 1, 3).reshape(64, 32, 128)
    keep, send, flat, weights = spectra_call(
        det, order, wigner, alm, beams, crossing, offsets.reshape(32, 128), fraction.reshape(32, 128), taps
    )
    partner = lax.ppermute(send, "det", [(0, 1), (1, 0)])
    message = (keep + partner).astype(BF16).reshape(ORD, ROWS, 2, 128)
    arrived = lax.all_to_all(message, "ord", split_axis=0, concat_axis=0, tiled=True)
    outgoing = circle_call(arrived.reshape(ORD * 2 * ROWS, 128))
    came = lax.all_to_all(outgoing, "ord", split_axis=0, concat_axis=0, tiled=True)
    return signal_call(flat, came, weights)


def solution(mesh):
    return jax.shard_map(
        local,
        mesh=mesh,
        in_specs=(
            P("ord", None, None, "det"),
            P("ord", None, None),
            P(),
            P("ord", None),
            P("ord", None),
            P("ord", None),
            P(),
        ),
        out_specs=P("det", "ord"),
        check_vma=False,
    )
```

```python
import math

import jax
import jax.numpy as jnp
import numpy as np
from jax import lax
from jax.experimental import pallas as pl
from jax.experimental.pallas import tpu as pltpu
from jax.sharding import PartitionSpec as P

F32 = jnp.float32
BF16 = jnp.bfloat16
I32 = jnp.int32

ORD = 128
ROWS = 9
NT = (((1,), (1,)), ((), ()))


def lanes_of(shape):
    return lax.broadcasted_iota(I32, shape, len(shape) - 1)


def near(x):
    return pltpu.with_memory_space_constraint(x, pltpu.VMEM)


def circulant(v):
    x = jnp.broadcast_to(v, (128, 128))
    sub = lax.broadcasted_iota(I32, (128, 128), 0)
    for bit in range(7):
        x = jnp.where((lax.shift_right_logical(sub, bit) & 1) == 1, pltpu.roll(x, 1 << bit, 1), x)
    return x


def two_parts(x):
    hi = x.astype(BF16)
    return hi, (x - hi.astype(F32)).astype(BF16)


def spectra_kernel(
    det_ref, ord_ref, wig_hbm, alm_hbm, beam_hbm, cross_hbm, offset_hbm, fraction_hbm, taps_hbm, keep, send, flat, weights,
    wig, alm, beam, crossing, offsets, fraction, taps, cells, wide, beams, product, found, sems,
):
    det = det_ref[0]
    half_lanes = pl.ds(pl.multiple_of(1024 * det, 1024), 1024)
    copies = [
        pltpu.make_async_copy(beam_hbm.at[:, pl.ds(pl.multiple_of(16 * det, 16), 16), :], beam, sems.at[8]),
        pltpu.make_async_copy(cross_hbm, crossing, sems.at[9]),
        pltpu.make_async_copy(offset_hbm, offsets, sems.at[10]),
        pltpu.make_async_copy(fraction_hbm, fraction, sems.at[11]),
        pltpu.make_async_copy(alm_hbm.at[:, :, half_lanes], alm, sems.at[12]),
    ]
    coefficients = pltpu.make_async_copy(taps_hbm, taps, sems.at[13])
    coefficients.start()
    block = lambda g: pltpu.make_async_copy(wig_hbm.at[pl.ds(2 * g, 2)], wig.at[pl.ds(2 * g, 2)], sems.at[g])
    for copy in copies:
        copy.start()
    for g in range(8):
        block(g).start()

    def build(slot, k, m):
        for half in range(2):
            for c in range(2):
                row = alm[m, c : c + 1, :]
                at = 64 * half + 32 * c
                product[slot, at : at + 32, :] = beams[k, 32 * half : 32 * half + 32, :] * row

    def prepare():
        copies[0].wait()
        wide[...] = beam[...].astype(F32).reshape(1024, 128)
        for half in range(2):
            base = (32 * det if half == 0 else 32 * (1 - det)) * 16
            for k in range(2):
                for t in range(8):
                    x = wide[pl.ds(base + 2 * t + k, 32, stride=16), :]
                    beams[k, 32 * half : 32 * half + 32, 128 * t : 128 * t + 128] = x.astype(BF16)
        for copy in copies[1:4]:
            copy.wait()
        c = crossing[...]
        holder = lax.shift_right_logical(c, 6)
        across = jnp.broadcast_to(holder, (128, 128)).astype(F32)
        down = jnp.transpose(across)
        sub = lax.broadcasted_iota(I32, (128, 128), 0)
        lane = lanes_of((128, 128))
        earlier = jnp.where((across == down) & (sub < lane), 1.0, 0.0)
        slot = jnp.sum(earlier, axis=0, keepdims=True).astype(I32)
        flat[0:1] = holder
        flat[1:2] = (32 * (lane[0:1] & 3) - 32 * slot) & 127
        o32 = offsets[...].astype(F32)
        f32_ = fraction[...]
        hi = f32_.astype(BF16).astype(F32)
        lo = f32_ - hi
        lane32 = lanes_of((32, 128))
        ids = jnp.broadcast_to((c & 63).astype(F32), (128, 128))
        ids = jnp.sum(jnp.where(sub == lane, ids, 0.0), axis=1, keepdims=True)
        end = ((lane < 112) & (sub == 0)) | ((lane >= 112) & (sub == 127))
        ids = jnp.broadcast_to(ids, (128, 128)) + jnp.where(end, 64.0, 0.0)
        for part in range(4):
            sh = 128 - 32 * part
            row = jnp.where(
                lane32 < 32,
                pltpu.roll(o32, sh % 128, 1),
                jnp.where(
                    lane32 < 64, pltpu.roll(hi, (sh + 32) % 128, 1), pltpu.roll(lo, (sh + 64) % 128, 1)
                ),
            )
            cells[pl.ds(part, 32, stride=4), :] = row
        data = jnp.where(lane < 96, cells[...], ids).astype(BF16)
        for s in range(2):
            pick = jnp.where((sub == holder) & (slot == s), 1.0, 0.0).astype(BF16)
            got = jnp.dot(pick, data, preferred_element_type=F32)
            keep[pl.ds(8 + 9 * s, 128, stride=18), :] = got
            send[pl.ds(8 + 9 * s, 128, stride=18), :] = jnp.zeros((128, 128), F32)

    lane = lanes_of((128, 128))

    def place(step, from_):
        first = jnp.where((ord_ref[0] == 0) & (step == 0), 1.0 / 64.0, 1.0 / 32.0)
        for k in range(2):
            one = found[from_ + 2 * k] * first
            two = found[from_ + 2 * k + 1] * (1.0 / 32.0)
            row = pl.ds(k * 1152 + step, 128, stride=9)
            keep[row, :] = jnp.where(lane < 64, one, pltpu.roll(two, 64, 1))
            send[row, :] = jnp.where(lane < 64, pltpu.roll(one, 64, 1), two)

    coefficients.wait()
    at = lanes_of((1, 128))
    v = jnp.zeros((1, 128), F32)
    for lag in range(33):
        v = jnp.where(at == (16 - lag) % 128, taps[lag], v)
    ring = circulant(v)
    gap = lanes_of((128, 128)) - lax.broadcasted_iota(I32, (128, 128), 0)
    near = (gap >= -64) & (gap <= 64)
    hi, lo = two_parts(jnp.concatenate([jnp.where(near, ring, 0.0), jnp.where(near, 0.0, ring)], axis=0))
    weights[...] = jnp.concatenate([hi, lo], axis=1)
    prepare()
    copies[4].wait()

    def step(t, carry):
        block(2 * t).wait()
        block(2 * t + 1).wait()
        for part in range(2):
            place(jnp.maximum(2 * t - 2, 0) + part, 4 * part)
        for unit in range(8):
            g, k, e = 2 * t + unit // 4, unit // 2 % 2, unit % 2
            build(unit % 4, k, 2 * g + e)
            found[unit] = lax.dot_general(wig[2 * g + e, k], product[unit % 4], NT, preferred_element_type=F32)
        return carry

    lax.fori_loop(0, 4, step, 0)
    place(6, 0)
    place(7, 4)


def spectra_call(det, order, wig, alm, beam, crossing, offsets, fraction, taps):
    smem = pl.BlockSpec(memory_space=pltpu.SMEM)
    vmem = pl.BlockSpec(memory_space=pltpu.VMEM)
    return pl.pallas_call(
        spectra_kernel,
        in_specs=[smem, smem] + [pl.BlockSpec(memory_space=pl.ANY)] * 7,
        out_specs=[vmem] * 4,
        out_shape=[
            pltpu.VMEM((2304, 128), F32),
            pltpu.VMEM((2304, 128), F32),
            jax.ShapeDtypeStruct((2, 128), I32),
            pltpu.VMEM((256, 256), BF16),
        ],
        scratch_shapes=[
            pltpu.VMEM((16, 2, 128, 1024), BF16),
            pltpu.VMEM((16, 2, 1024), BF16),
            pltpu.VMEM((64, 16, 128), BF16),
            pltpu.VMEM((1, 128), I32),
            pltpu.VMEM((32, 128), I32),
            pltpu.VMEM((32, 128), F32),
            pltpu.SMEM((33,), F32),
            pltpu.VMEM((128, 128), F32),
            pltpu.VMEM((1024, 128), F32),
            pltpu.VMEM((2, 64, 1024), BF16),
            pltpu.VMEM((4, 128, 1024), BF16),
            pltpu.VMEM((8, 128, 128), F32),
            pltpu.SemaphoreType.DMA((14,)),
        ],
        name="spectra",
    )(det, order, wig, alm, beam, crossing, offsets, fraction, taps)


def tables():
    d = np.arange(128)[:, None]
    p = np.arange(256)[None, :]
    here = 2.0 * np.pi * ((d * p) % 256) / 256.0
    after = 2.0 * np.pi * (((d + 1) * p) % 256) / 256.0
    eighth = here + 2.0 * np.pi * 8 * p / 4096.0
    cat = np.concatenate
    real = cat([np.cos(here), -np.sin(here), np.cos(after), -np.sin(after)], axis=0)
    imag = cat([np.sin(here), np.cos(here), -np.sin(after), -np.cos(after)], axis=0)
    folded = cat([real, imag], axis=1)
    ends = cat([cat([np.cos(x), -np.sin(x)], axis=0) for x in (here, eighth)], axis=1)
    turn = 2.0 * np.pi * np.arange(8)[:, None] * p / 4096.0
    small = lambda x: x.astype(np.float32).astype(BF16)
    return small(folded), small(ends), np.cos(turn).astype(np.float32), np.sin(turn).astype(np.float32)


def real_dft16(a, b):
    c = math.sqrt(0.5)
    c1, c3 = math.cos(math.pi / 8), math.cos(3 * math.pi / 8)
    s1, s3 = math.sin(math.pi / 8), math.sin(3 * math.pi / 8)
    p08, m08 = a[0] + a[8], a[0] - a[8]
    s26, d26 = a[2] + a[6], (a[2] - a[6]) * c
    s17, d17, s35, d35 = a[1] + a[7], a[1] - a[7], a[3] + a[5], a[3] - a[5]
    even = [p08 + a[4] + s26, m08 + d26, p08 - a[4], m08 - d26, p08 + a[4] - s26]
    odd = [s17 + s35, d17 * c1 + d35 * c3, (s17 - s35) * c, d17 * c3 - d35 * c1]
    cosine = [None] * 9
    for p in range(4):
        cosine[p] = even[p] + odd[p]
        cosine[8 - p] = even[p] - odd[p]
    cosine[4] = even[4]
    t17, u17, t35, u35 = b[1] + b[7], b[1] - b[7], b[3] + b[5], b[3] - b[5]
    t26, u26 = (b[2] + b[6]) * c, b[2] - b[6]
    bo = [None, t17 * s1 + t35 * s3, (u17 + u35) * c, t17 * s3 - t35 * s1]
    be = [None, t26 + b[4], u26, t26 - b[4]]
    sine = [None] * 8
    for p in range(1, 4):
        sine[p] = bo[p] + be[p]
        sine[8 - p] = bo[p] - be[p]
    sine[4] = u17 - u35
    out = [None] * 16
    out[0], out[8] = cosine[0], cosine[8]
    for p in range(1, 8):
        out[p] = cosine[p] - sine[p]
        out[16 - p] = cosine[p] + sine[p]
    return out


def lagrange_weights(position):
    shifted = position + 1.0
    minus_one = position - 1.0
    minus_two = position - 2.0
    return (
        -position * minus_one * minus_two / 6.0,
        shifted * minus_one * minus_two / 2.0,
        -shifted * position * minus_two / 2.0,
        shifted * position * minus_one / 6.0,
    )


def circle_kernel(
    got, folded, single, tcos, tsin, out,
    wide, left, left0, left8, field, field0, field8, tiles, grid_o, grid_w, ends, mark, ids_v, ids_s, sem,
):
    wide[...] = got[...].astype(F32)
    for s in range(2):
        flipped = jnp.transpose(wide[pl.ds(8 + 9 * s, 128, stride=18), :])
        ids_v[8 * s : 8 * s + 8, :] = flipped[96:104, :].astype(I32) & 63
    copy = pltpu.make_async_copy(ids_v, ids_s, sem)
    copy.start()
    for i in range(2):
        for g in range(8):
            flipped = jnp.transpose(wide[pl.ds(9 * i + g, 128, stride=18), :].astype(BF16))
            for odd in range(2):
                e = 2 * g + odd
                if e % 8 == 0:
                    to, row, lane0 = (left0 if e == 0 else left8), 32 * i, 0
                else:
                    to, row, lane0 = left, (min(e, 16 - e) - 1) * 64 + 32 * i, 0 if e < 8 else 256
                to[row : row + 32, lane0 : lane0 + 128] = flipped[64 * odd : 64 * odd + 32]
                to[row : row + 32, lane0 + 128 : lane0 + 256] = flipped[64 * odd + 32 : 64 * odd + 64]
    field[...] = jnp.dot(left[...], folded[...], preferred_element_type=F32)
    field0[...] = jnp.dot(left0[...], single[:, 0:256], preferred_element_type=F32)
    field8[...] = jnp.dot(left8[...], single[:, 256:512], preferred_element_type=F32)
    for half in range(2):
        re = slice(128 * half, 128 * half + 128)
        im = slice(256 + 128 * half, 256 + 128 * half + 128)
        for r in range(4):
            a, b = [field0[16 * r : 16 * r + 16, re]], [None]
            for e in range(1, 8):
                row = slice(64 * (e - 1) + 16 * r, 64 * (e - 1) + 16 * r + 16)
                yr, yi = field[row, re], field[row, im]
                tc, ts = tcos[e : e + 1, re], tsin[e : e + 1, re]
                a.append(yr * tc - yi * ts)
                b.append(yr * ts + yi * tc)
            a.append(field8[16 * r : 16 * r + 16, re])
            i, j = r // 2, r % 2
            for p, x in enumerate(real_dft16(a, b)):
                tiles[32 * i + 2 * p + half, 16 * j : 16 * j + 16, :] = x.astype(BF16)
    part = lanes_of((64, 128)) // 32
    o = jnp.zeros((64, 128), F32)
    f = jnp.zeros((64, 128), F32)
    for n in range(2):
        for s in range(2):
            x = wide[pl.ds(18 * n + 8 + 9 * s, 64, stride=36), :]
            to = 2 * n + s
            o = jnp.where(part == to, pltpu.roll(x, 32 * to, 1), o)
            y = x + pltpu.roll(x, 96, 1)
            f = jnp.where(part == to, pltpu.roll(y, (32 * to + 96) % 128, 1), f)
    grid_o[...] = o
    for place, w in enumerate(lagrange_weights(f)):
        grid_w[place] = w
    part = lanes_of((128, 128)) // 32
    one = wide[pl.ds(8, 128, stride=18), :]
    two = wide[pl.ds(17, 128, stride=18), :]
    mark[...] = jnp.where(
        part < 2,
        jnp.where(part == 0, pltpu.roll(one, 32, 1), pltpu.roll(two, 64, 1)),
        jnp.where(part == 2, pltpu.roll(one, 96, 1), two),
    )
    ends[0] = jnp.zeros((8, 128), F32)
    ends[129] = jnp.zeros((8, 128), F32)
    copy.wait()
    sub = lax.broadcasted_iota(I32, (128, 128), 0).astype(F32).astype(BF16)
    lane32 = lanes_of((32, 128)) // 32
    low16 = lanes_of((16, 128)) < 64
    even8 = (lanes_of((8, 128)) // 32) % 2 == 0

    def pair(t, carry):
        row = lambda ref: jnp.broadcast_to(ref[pl.ds(t, 1), :], (128, 128)).astype(BF16)
        distance = sub - row(grid_o)
        matrix = jnp.zeros((128, 128), BF16)
        for place in range(4):
            matrix = jnp.where(distance == place, row(grid_w.at[place]), matrix)
        stack = jnp.concatenate(
            [tiles[ids_s[8 * s, 2 * t + n]] for n in range(2) for s in range(2)], axis=0
        )
        res = jnp.dot(stack, matrix, preferred_element_type=F32)
        d = res[0:32]
        for q in range(1, 4):
            d = jnp.where(lane32 == q, res[32 * q : 32 * q + 32], d)
        a, b = d[0:16], d[16:32]
        for n in range(2):
            m = 2 * t + n
            x = jnp.where(low16, a, pltpu.roll(b, 64, 1)) if n == 0 else jnp.where(low16, pltpu.roll(a, 64, 1), b)
            out[m, 0:16, :] = x.astype(BF16)
            x = jnp.where(mark[pl.ds(m, 1), :] >= 64.0, x, 0.0)
            x = x + pltpu.roll(x, 96, 1)
            ends[m + 1] = jnp.where(even8, x[0:8], pltpu.roll(x[8:16], 32, 1))
        return carry

    lax.fori_loop(0, 64, pair, 0, unroll=64)
    tail = lanes_of((8, 128)) % 32 >= 16

    def rims(n, carry):
        out[n, 16:24, :] = jnp.where(tail, ends[n], ends[n + 2]).astype(BF16)
        return carry

    lax.fori_loop(0, 128, rims, 0, unroll=16)


def circle_call(got):
    folded, single, tcos, tsin = tables()
    vmem = pl.BlockSpec(memory_space=pltpu.VMEM)
    return pl.pallas_call(
        circle_kernel,
        in_specs=[vmem] * 5,
        out_specs=vmem,
        out_shape=pltpu.VMEM((128, 24, 128), BF16),
        scratch_shapes=[
            pltpu.VMEM((2304, 128), F32),
            pltpu.VMEM((448, 512), BF16),
            pltpu.VMEM((64, 256), BF16),
            pltpu.VMEM((64, 256), BF16),
            pltpu.VMEM((448, 512), F32),
            pltpu.VMEM((64, 256), F32),
            pltpu.VMEM((64, 256), F32),
            pltpu.VMEM((64, 32, 128), BF16),
            pltpu.VMEM((64, 128), F32),
            pltpu.VMEM((4, 64, 128), F32),
            pltpu.VMEM((130, 8, 128), F32),
            pltpu.VMEM((128, 128), F32),
            pltpu.VMEM((16, 128), I32),
            pltpu.SMEM((16, 128), I32),
            pltpu.SemaphoreType.DMA,
        ],
        name="circle",
    )(near(got), *[near(jnp.asarray(x)) for x in (folded, single, tcos, tsin)])


def signal_kernel(flat_any, came, weights, out_any, flat, line, result, out, sems):
    slots = pltpu.make_async_copy(flat_any, flat, sems.at[4])
    slots.start()
    lane = lanes_of((16, 128)) // 32
    lane32 = lanes_of((32, 128))

    def add(h, total):
        return total + came[h, 16:24, :].astype(F32)

    total = lax.fori_loop(0, 128, add, jnp.zeros((8, 128), F32), unroll=16)
    rim = jnp.concatenate([total] + [pltpu.roll(total, 128 - 32 * j, 1) for j in range(1, 4)], axis=0)
    before = pltpu.roll(rim, 96, 1).astype(BF16)
    after = rim.astype(BF16)

    slots.wait()

    def block(b, carry):
        older, newer = carry
        low = jnp.zeros((16, 128), F32)
        high = jnp.zeros((16, 128), F32)
        for q in range(4):
            x = came[flat[0, 4 * b + q], 0:16, :].astype(F32)
            shift = flat[1, 4 * b + q]
            low = jnp.where(lane == q, pltpu.roll(x, shift, 1), low)
            high = jnp.where(lane == q, pltpu.roll(x, shift ^ 64, 1), high)
        x = jnp.concatenate([low, high], axis=0).astype(BF16)
        line[b + 1, :, 0:128] = x
        line[b, :, 128:256] = jnp.where(lane32 < 64, x, older)
        return newer, x

    older, newer = lax.fori_loop(0, 32, block, (jnp.zeros((32, 128), BF16), before), unroll=32)
    line[32, :, 128:256] = jnp.where(lane32 < 64, after, older)
    copies = []
    for part in range(4):
        result[...] = jnp.dot(
            line[1 + 8 * part : 9 + 8 * part].reshape(256, 256), weights[...], preferred_element_type=F32
        )
        for b in range(8):
            y = result[32 * b : 32 * b + 32, :]
            out[part, :, 128 * b : 128 * b + 128] = y[:, 0:128] + y[:, 128:256]
        copies.append(
            pltpu.make_async_copy(out.at[part], out_any.at[:, pl.ds(1024 * part, 1024)], sems.at[part])
        )
        copies[-1].start()
    for copy in copies:
        copy.wait()


def signal_call(flat, came, weights):
    vmem = pl.BlockSpec(memory_space=pltpu.VMEM)
    return pl.pallas_call(
        signal_kernel,
        in_specs=[pl.BlockSpec(memory_space=pl.ANY), vmem, vmem],
        out_specs=pl.BlockSpec(memory_space=pl.ANY),
        out_shape=jax.ShapeDtypeStruct((32, 4096), F32),
        scratch_shapes=[
            pltpu.SMEM((2, 128), I32),
            pltpu.VMEM((33, 32, 256), BF16),
            pltpu.VMEM((256, 256), F32),
            pltpu.VMEM((4, 32, 1024), F32),
            pltpu.SemaphoreType.DMA((5,)),
        ],
        name="signal",
    )(flat, near(came), near(weights))


def local(wigner, alm, beam, crossing, offsets, fraction, taps):
    det = lax.axis_index("det").astype(I32).reshape(1)
    order = lax.axis_index("ord").astype(I32).reshape(1)
    beams = beam.reshape(64, 2, 16, 128).transpose(0, 2, 1, 3).reshape(64, 32, 128)
    keep, send, flat, weights = spectra_call(
        det, order, wigner, alm, beams, crossing, offsets.reshape(32, 128), fraction.reshape(32, 128), taps
    )
    partner = lax.ppermute(send, "det", [(0, 1), (1, 0)])
    message = (keep + partner).astype(BF16).reshape(ORD, ROWS, 2, 128)
    arrived = lax.all_to_all(message, "ord", split_axis=0, concat_axis=0, tiled=True)
    outgoing = circle_call(arrived.reshape(ORD * 2 * ROWS, 128))
    came = lax.all_to_all(outgoing, "ord", split_axis=0, concat_axis=0, tiled=True)
    return signal_call(flat, came, weights)


def solution(mesh):
    return jax.shard_map(
        local,
        mesh=mesh,
        in_specs=(
            P("ord", None, None, "det"),
            P("ord", None, None),
            P(),
            P("ord", None),
            P("ord", None),
            P("ord", None),
            P(),
        ),
        out_specs=P("det", "ord"),
        check_vma=False,
    )
```
